512 devices in a mesh: state: 8 (over y), mode: 64 (over z, x, core).
Axes of the slice: x: 4, y: 8, z: 8, core: 2. Of those that a mesh axis runs over, the one named last changes fastest.
Arguments:
- coeffs: float32 [8, 512, 4096], P('state', 'mode'), may hold values from -0.375 to 0.375
- diag_h2: float32 [8, 32, 4096], P('state'), may hold values from -0.75 to 0.75
- diag_h3: float32 [8, 32, 4096], P('state'), may hold values from -0.75 to 0.75
- diag_v1: float32 [8, 32, 512], P('state', None, 'mode'), may hold values from -1.5 to 1.5
- coup_h2: float32 [32, 4096], replicated, may hold values from -0.75 to 0.75
- coup_h3: float32 [32, 4096], replicated, may hold values from -0.75 to 0.75
- coup_v1: float32 [32, 512], P(None, 'mode'), may hold values from -1.5 to 1.5
- pairs: int32 [128, 3], replicated, may hold values from 0 to 31, as said below
Outputs:
- action: float32 [8, 512, 4096], P('state', 'mode')
- diag_field: float32 [8, 64, 2048], P('state', 'mode')
- pair_field: float32 [8, 64, 3072], P('state', 'mode')
The draws below stay inside these ranges and needn't reach their ends.
Inputs may be any that keep to these rules, and one draw needn't show every extreme that they name: `pairs`: each row is (target state, source state, coupling term); the source differs from the target; every state is the target of at most 48 rows, and one state of exactly 48.
All inputs are finite; a program needn't handle non-finite values.
Results may differ from the reference program's by a relative error of at most 0.0001.
Values sent between devices are 32-bit elements; how exact they have to be, the bound alone decides.
No kernel may reach another device: no remote copies, remote signals or barrier semaphores. Data moves between devices by JAX's collectives and lax.ppermute only.
A program may use at most 64 MiB of HBM per device.

```python
import jax
import jax.numpy as jnp
from jax import lax

N2 = 64
N3 = 64
NDIAG = 32
NCOUP = 32
STATES = 8
G1 = 512
NPAIRS = 128
MAXP = 48


def draw_pairs(key, part):
    subkeys = jax.random.split(key, 5)
    order_states = jax.random.permutation(subkeys[0], STATES).astype(jnp.int32)
    remaining = NPAIRS - MAXP
    half_count = remaining // 2
    crowded = jnp.full((MAXP,), order_states[0], jnp.int32)
    spread = order_states[1 + jnp.arange(half_count, dtype=jnp.int32) % (STATES - 1)]
    random_part = order_states[1 + jax.random.randint(subkeys[1], (remaining - half_count,), 0, STATES - 1)]
    targets = jnp.concatenate([crowded, spread, random_part]).astype(jnp.int32)
    targets = targets[jax.random.permutation(subkeys[2], NPAIRS)]
    sources = (targets + jax.random.randint(subkeys[3], (NPAIRS,), 1, STATES)) % STATES
    term_ids = jax.random.randint(subkeys[4], (NPAIRS,), 0, NCOUP)
    return jnp.stack([targets, sources.astype(jnp.int32), term_ids.astype(jnp.int32)], axis=1).astype(jnp.int32)


def block_scale(key, dims, cuts, least, top_value):
    level, own = 1.0, jax.random.fold_in(key, 6)
    for dim, blocks in cuts:
        heights = jnp.exp(jax.random.uniform(jax.random.fold_in(own, dim), (blocks,), jnp.float32, least / len(cuts), top_value / len(cuts)))
        level = level * jnp.repeat(heights, dims[dim] // blocks).reshape([-1 if axis == dim else 1 for axis in range(len(dims))])
    return level


def normal_values(own_key, extent, scale, most, pieces=(), kind=jnp.bfloat16):
    drawn = jax.random.normal(own_key, extent, jnp.float32) * scale
    if len(pieces) > 0:
        drawn = block_scale(own_key, extent, pieces, -0.22, 0.18) * drawn
    return jnp.clip(drawn, min=-most, max=most).astype(kind)


def setup_inputs(seed: int = 0) -> dict:
    keys = jax.random.split(jax.random.key(seed), 9)
    coeffs = normal_values(keys[0], (STATES, G1, N2 * N3), (4 * N3) ** -0.5, 0.375, ((0, 8), (1, 64)), jnp.float32)
    diag_h2 = normal_values(keys[1], (STATES, NDIAG, N2 * N2), N2 ** -0.5, 0.75, ((0, 8),), jnp.float32)
    diag_h3 = normal_values(keys[2], (STATES, NDIAG, N3 * N3), N3 ** -0.5, 0.75, ((0, 8),), jnp.float32)
    diag_v1 = jnp.clip(jax.random.uniform(keys[3], (STATES, NDIAG, G1), jnp.float32, -1.5, 1.5) * block_scale(keys[3], (STATES, NDIAG, G1), ((0, 8), (2, 64)), -0.4, 0.0), -1.5, 1.5)
    coup_h2 = normal_values(keys[4], (NCOUP, N2 * N2), N2 ** -0.5, 0.75, (), jnp.float32)
    coup_h3 = normal_values(keys[5], (NCOUP, N3 * N3), N3 ** -0.5, 0.75, (), jnp.float32)
    coup_v1 = jnp.clip(jax.random.uniform(keys[6], (NCOUP, G1), jnp.float32, -1.5, 1.5) * block_scale(keys[6], (NCOUP, G1), ((1, 64),), -0.4, 0.0), -1.5, 1.5)
    pairs = draw_pairs(jax.random.fold_in(keys[8], 71), 0)
    return {"coeffs": coeffs, "diag_h2": diag_h2, "diag_h3": diag_h3, "diag_v1": diag_v1, "coup_h2": coup_h2, "coup_h3": coup_h3, "coup_v1": coup_v1, "pairs": pairs}


HIGH = lax.Precision.HIGHEST


def reference(coeffs, diag_h2, diag_h3, diag_v1, coup_h2, coup_h3, coup_v1, pairs):
    tensors = coeffs.reshape(STATES, G1, N2, N3)
    diag_h2 = diag_h2.reshape(STATES, NDIAG, N2, N2)
    diag_h3 = diag_h3.reshape(STATES, NDIAG, N3, N3)
    coup_h2 = coup_h2.reshape(NCOUP, N2, N2)
    coup_h3 = coup_h3.reshape(NCOUP, N3, N3)
    actions = []
    diag_list = []
    for state_index in range(STATES):
        tensor = tensors[state_index]

        def diag_term(accumulated, inputs, tensor=tensor):
            left_op, right_op, weights = inputs
            product = jnp.einsum('gac,dc->gad', tensor, right_op, precision=HIGH)
            action = jnp.einsum('ea,gad->ged', left_op, product, precision=HIGH) * weights[:, None, None]
            weighted = tensor * weights[:, None, None]
            field_block = jnp.einsum('gac,gbc->ab', weighted, product, precision=HIGH)
            return accumulated + action, field_block

        accumulated, fields = lax.scan(diag_term, jnp.zeros((G1, N2, N3), jnp.float32),
                                       (diag_h2[state_index], diag_h3[state_index], diag_v1[state_index]))
        actions.append(accumulated)
        diag_list.append(fields)
    action_all = jnp.stack(actions)
    diag_fields = jnp.stack(diag_list)
    targets = pairs[:, 0]
    positions = jnp.arange(NPAIRS, dtype=jnp.int32)
    earlier_same = (targets[:, None] == targets[None, :]) & (positions[None, :] < positions[:, None])
    slot_ranks = jnp.sum(earlier_same.astype(jnp.int32), axis=1).astype(jnp.int32)

    def pair_term(carried, inputs):
        action_sum, pair_fields = carried
        target_id, source_id, term_id, slot_rank = inputs
        product = jnp.einsum('gac,dc->gad', tensors[source_id], coup_h3[term_id], precision=HIGH)
        weights = coup_v1[term_id]
        action = jnp.einsum('ea,gad->ged', coup_h2[term_id], product, precision=HIGH) * weights[:, None, None]
        weighted = tensors[target_id] * weights[:, None, None]
        field_block = jnp.einsum('gac,gbc->ab', weighted, product, precision=HIGH)
        action_sum = action_sum.at[target_id].add(action)
        pair_fields = pair_fields.at[target_id, slot_rank].set(field_block)
        return (action_sum, pair_fields), None

    start_fields = jnp.zeros((STATES, MAXP, N2, N2), jnp.float32)
    (action_all, pair_fields), _ = lax.scan(pair_term, (action_all, start_fields),
                                            (pairs[:, 0], pairs[:, 1], pairs[:, 2], slot_ranks))
    action = action_all.reshape(STATES, G1, N2 * N3)
    diag_field = diag_fields.transpose(0, 2, 1, 3).reshape(STATES, N2, NDIAG * N2)
    pair_field = pair_fields.transpose(0, 2, 1, 3).reshape(STATES, N2, MAXP * N2)
    return (action, diag_field, pair_field)
```

```python
import jax
import jax.numpy as jnp
from jax import lax
from jax.experimental import pallas as pl
from jax.experimental.pallas import tpu as pltpu
from jax.sharding import Mesh, PartitionSpec as P

N = 64
G = 8
TERMS = 32
STATES = 8
SLOTS = 48
F32 = jnp.float32
BF16 = jnp.bfloat16
NT = (((1,), (1,)), ((), ()))
VMEM = pl.BlockSpec(memory_space=pltpu.VMEM)
SMEM = pl.BlockSpec(memory_space=pltpu.SMEM)


def dot(left, right):
    return jnp.dot(left, right, preferred_element_type=F32)


def dot_nt(left, right):
    return lax.dot_general(left, right, NT, preferred_element_type=F32)


def split(value):
    high = value.astype(BF16)
    low = (value - high.astype(F32)).astype(BF16)
    return high, low


def split_lanes(value):
    return jnp.concatenate(split(value), axis=1)


def half_blocks(operator):
    left = lax.broadcasted_iota(jnp.int32, operator.shape, 1) < N
    high = operator.astype(BF16).astype(F32)
    low = operator - high
    zero = jnp.zeros_like(operator)
    return [
        jnp.where(left, high, zero).astype(BF16),
        jnp.where(left, zero, high).astype(BF16),
        jnp.where(left, low, zero).astype(BF16),
        jnp.where(left, zero, low).astype(BF16),
    ]


def tile_nt(operator):
    h0, h1, l0, l1 = half_blocks(operator)
    zero = jnp.zeros((2 * N, 2 * N), BF16)
    high = jnp.concatenate([h0, h1], axis=0)
    low = jnp.concatenate([l0, l1], axis=0)
    return jnp.concatenate(
        [jnp.concatenate([high, low], axis=0), jnp.concatenate([high, zero], axis=0)], axis=1
    )


def tile_nn(operator):
    h0, h1, l0, l1 = half_blocks(operator)
    zero = jnp.zeros((2 * N, 2 * N), BF16)
    high = jnp.concatenate([h0, h1], axis=0)
    low = jnp.concatenate([l0, l1], axis=0)
    return jnp.concatenate(
        [jnp.concatenate([high, low], axis=1), jnp.concatenate([high, zero], axis=1)], axis=0
    )


def put_term(product, weight, index, high_ref, low_ref):
    value = product[:, : 2 * N] + product[:, 2 * N :]
    rows = pl.ds(pl.multiple_of(index * N, N), N)
    for pair in range(G // 2):
        part = value[pair * N : (pair + 1) * N] * weight[pair : pair + 1]
        high, low = split(part)
        high_ref[rows, pair * 2 * N : (pair + 1) * 2 * N] = high
        low_ref[rows, pair * 2 * N : (pair + 1) * 2 * N] = low


def act_on(left_ref, high_ref, low_ref):
    high, low = split(left_ref[...])
    both = dot(jnp.concatenate([high, low], axis=0), high_ref[...])
    return both[:N] + both[N:] + dot(high, low_ref[...])


def own_kernel(a_ref, ap_ref, h3_ref, h2_ref, v_ref, c3_ref, cv_ref,
               act_ref, mine_ref, other_ref, zh_ref, zl_ref, wh_ref, wl_ref):
    left = split_lanes(a_ref[...])

    def own_term(t, carry):
        put_term(dot_nt(left, tile_nt(h3_ref[t])), v_ref[t], t, wh_ref, wl_ref)
        return carry

    lax.fori_loop(0, TERMS, own_term, 0)
    act_ref[...] = act_on(h2_ref, wh_ref, wl_ref)

    wide = jnp.concatenate([ap_ref[p * N : (p + 1) * N, :] for p in range(G // 2)], axis=1)
    high, low = split(wide)
    rows_both = jnp.concatenate([high, low], axis=0)
    for j in range(TERMS // 4):
        part = slice(j * 4 * N, (j + 1) * 4 * N)
        both = dot_nt(rows_both, wh_ref[part, :])
        field = both[:N] + both[N:] + dot_nt(high, wl_ref[part, :])
        for half in range(2):
            lanes = slice(half * 2 * N, (half + 1) * 2 * N)
            where_to = pl.ds(2 * j + half, N // 2, stride=TERMS // 2)
            mine_ref[where_to, :] = field[: N // 2, lanes]
            other_ref[where_to, :] = field[N // 2 :, lanes]

    left_p = split_lanes(ap_ref[...])

    def coupling_term(k, carry):
        put_term(dot(left_p, tile_nn(c3_ref[k])), cv_ref[k], k, zh_ref, zl_ref)
        return carry

    lax.fori_loop(0, TERMS, coupling_term, 0)


def field_kernel(source_ref, term_ref, valid_ref, all_ref, zh_ref, zl_ref,
                 mine_ref, other_ref, gh_ref, gl_ref, f_ref):
    for q in range(STATES):
        for pair in range(G // 2):
            high, low = split(all_ref[q, pair * N : (pair + 1) * N, :])
            lanes = slice(pair * 2 * N, (pair + 1) * 2 * N)
            gh_ref[q * N : (q + 1) * N, lanes] = high
            gl_ref[q * N : (q + 1) * N, lanes] = low

    def block(j, carry):
        rows = pl.ds(pl.multiple_of(j * 4 * N, 4 * N), 4 * N)
        zh = zh_ref[rows, :]
        left = jnp.concatenate([zh, zl_ref[rows, :], zh], axis=1)
        for half in range(2):
            here = slice(half * 4 * N, (half + 1) * 4 * N)
            gh = gh_ref[here, :]
            right = jnp.concatenate([gh, gh, gl_ref[here, :]], axis=1)
            product = dot_nt(left, right)
            f_ref[2 * half, rows, :] = product[:, : 2 * N]
            f_ref[2 * half + 1, rows, :] = product[:, 2 * N :]
        return carry

    lax.fori_loop(0, TERMS // 4, block, 0)
    is_left = lax.broadcasted_iota(jnp.int32, (N, 2 * N), 1) < N

    def pick(slot):
        source = source_ref[slot]
        rows = pl.ds(pl.multiple_of(term_ref[slot] * N, N), N)
        return f_ref[source // 2, rows, :], lax.rem(source, 2)

    def slot_pair(i, carry):
        first, odd_first = pick(2 * i)
        second, odd_second = pick(2 * i + 1)
        first = jnp.where(odd_first == 1, pltpu.roll(first, N, 1), first)
        second = jnp.where(odd_second == 0, pltpu.roll(second, N, 1), second)
        first = jnp.where(valid_ref[2 * i] == 1, first, 0.0)
        second = jnp.where(valid_ref[2 * i + 1] == 1, second, 0.0)
        field = jnp.where(is_left, first, second)
        where_to = pl.ds(i, N // 2, stride=SLOTS // 2)
        mine_ref[where_to, :] = field[: N // 2]
        other_ref[where_to, :] = field[N // 2 :]
        return carry

    lax.fori_loop(0, SLOTS // 2, slot_pair, 0)


def pair_kernel(count_ref, all_ref, c3_ref, c2_ref, cv_ref, act_ref, out_ref, wh_ref, wl_ref):
    def coupling_term(k, carry):
        total = all_ref[0] * count_ref[k, 0]
        for q in range(1, STATES):
            total = total + all_ref[q] * count_ref[k, q]
        put_term(dot_nt(split_lanes(total), tile_nt(c3_ref[k])), cv_ref[k], k, wh_ref, wl_ref)
        return carry

    lax.fori_loop(0, TERMS, coupling_term, 0)
    out_ref[...] = act_ref[...] + act_on(c2_ref, wh_ref, wl_ref)


def cost(flops, nbytes):
    return pl.CostEstimate(flops=flops, bytes_accessed=nbytes, transcendentals=0)


def own_part(a2, a2p, h3, h2, v, c3, cv):
    return pl.pallas_call(
        own_kernel,
        out_shape=(
            jax.ShapeDtypeStruct((N, G * N), F32),
            jax.ShapeDtypeStruct((N // 2 * TERMS // 2, 2 * N), F32),
            jax.ShapeDtypeStruct((N // 2 * TERMS // 2, 2 * N), F32),
            jax.ShapeDtypeStruct((TERMS * N, G * N), BF16),
            jax.ShapeDtypeStruct((TERMS * N, G * N), BF16),
        ),
        in_specs=[VMEM] * 7,
        out_specs=[VMEM] * 5,
        scratch_shapes=[pltpu.VMEM((TERMS * N, G * N), BF16)] * 2,
        compiler_params=pltpu.CompilerParams(vmem_limit_bytes=28 << 20),
        cost_estimate=cost(3_000_000_000, 8 << 20),
        name="own_part",
    )(a2, a2p, h3, h2, v, c3, cv)


def pair_fields(source, term, valid, everyone, zh, zl):
    rows = N // 2 * SLOTS // 2
    return pl.pallas_call(
        field_kernel,
        out_shape=(
            jax.ShapeDtypeStruct((rows, 2 * N), F32),
            jax.ShapeDtypeStruct((rows, 2 * N), F32),
        ),
        in_specs=[SMEM] * 3 + [VMEM] * 3,
        out_specs=[VMEM] * 2,
        scratch_shapes=[
            pltpu.VMEM((STATES * N, G * N), BF16),
            pltpu.VMEM((STATES * N, G * N), BF16),
            pltpu.VMEM((STATES // 2, TERMS * N, 2 * N), F32),
        ],
        compiler_params=pltpu.CompilerParams(vmem_limit_bytes=28 << 20),
        cost_estimate=cost(3_000_000_000, 6 << 20),
        name="pair_fields",
    )(source, term, valid, everyone, zh, zl)


def pair_action(count, everyone, c3, c2, cv, act):
    return pl.pallas_call(
        pair_kernel,
        out_shape=jax.ShapeDtypeStruct((N, G * N), F32),
        in_specs=[SMEM] + [VMEM] * 5,
        out_specs=VMEM,
        scratch_shapes=[pltpu.VMEM((TERMS * N, G * N), BF16)] * 2,
        compiler_params=pltpu.CompilerParams(vmem_limit_bytes=28 << 20),
        cost_estimate=cost(3_000_000_000, 4 << 20),
        name="pair_action",
    )(count, everyone, c3, c2, cv, act)


def twice(flat):
    matrices = flat.reshape(TERMS, N, N)
    return jnp.concatenate([matrices, matrices], axis=2)


def rows_by_term(flat):
    return flat.reshape(TERMS, N, N).transpose(1, 0, 2).reshape(N, TERMS * N)


def lane_weights(v):
    return jnp.repeat(v, N, axis=1).reshape(TERMS, G // 2, 2 * N)


def arrange(coeffs, core):
    tensor = coeffs.reshape(G // 2, 2, N, N)
    plain = tensor.transpose(0, 2, 1, 3).reshape(G // 2 * N, 2 * N)
    rows = plain.reshape(G // 2, N // 2, 2, 2 * N)
    even, odd = rows[:, :, 0], rows[:, :, 1]
    first = jnp.where(core == 0, even, odd)
    second = jnp.where(core == 0, odd, even)
    return plain, jnp.concatenate([first, second], axis=1).reshape(G // 2 * N, 2 * N)


def read_list(pairs, myself):
    is_mine = pairs[:, 0] == myself
    rank = jnp.cumsum(is_mine.astype(jnp.int32)) - 1
    slots = jnp.arange(SLOTS, dtype=jnp.int32)
    picked = (rank[None, :] == slots[:, None]) & is_mine[None, :]
    source = jnp.sum(jnp.where(picked, pairs[None, :, 1], 0), axis=1)
    term = jnp.sum(jnp.where(picked, pairs[None, :, 2], 0), axis=1)
    valid = jnp.sum(picked.astype(jnp.int32), axis=1)
    by_term = (pairs[None, :, 2] == jnp.arange(TERMS, dtype=jnp.int32)[:, None]) & is_mine[None, :]
    by_source = pairs[None, :, 1] == jnp.arange(STATES, dtype=jnp.int32)[:, None]
    count = jnp.sum((by_term[:, None, :] & by_source[None, :, :]).astype(F32), axis=2)
    return source, term, valid, count


def per_device(coeffs, diag_h2, diag_h3, diag_v1, coup_h2, coup_h3, coup_v1, pairs):
    core = lax.axis_index("core")
    plain, mine_first = arrange(coeffs[0], core)
    everyone = lax.all_to_all(
        jnp.broadcast_to(plain[None], (STATES,) + plain.shape), "state", 0, 0, tiled=True
    )
    source, term, valid, count = read_list(pairs, lax.axis_index("state"))
    c3 = twice(coup_h3)
    cv = lane_weights(coup_v1)
    act, diag_mine, diag_other, zh, zl = own_part(
        plain, mine_first, twice(diag_h3[0]), rows_by_term(diag_h2[0]),
        lane_weights(diag_v1[0]), c3, cv,
    )
    swap = [(0, 1), (1, 0)]
    diag_sum = diag_mine + lax.ppermute(diag_other, "core", swap)
    pair_mine, pair_other = pair_fields(source, term, valid, everyone, zh, zl)
    pair_sum = pair_mine + lax.ppermute(pair_other, "core", swap)
    sums = jnp.concatenate(
        [diag_sum.reshape(N // 2, TERMS // 2, 2 * N), pair_sum.reshape(N // 2, SLOTS // 2, 2 * N)],
        axis=1,
    )
    parts = lax.all_to_all(sums, ("z", "x"), 0, 0, tiled=True)
    act = pair_action(count, everyone, c3, rows_by_term(coup_h2), cv, act)
    action = act.reshape(N, G, N).transpose(1, 0, 2).reshape(1, G, N * N)
    row = jnp.sum(parts, axis=0)
    diag_row = row[: TERMS // 2].reshape(1, 1, TERMS * N)
    pair_row = row[TERMS // 2 :].reshape(1, 1, SLOTS * N)
    return action, diag_row, pair_row


def solution(mesh):
    devices = mesh.devices
    fine = Mesh(devices.reshape(8, 8, 4, 2), ("state", "z", "x", "core"))
    mode = ("z", "x", "core")
    placed = (
        P("state", mode, None),
        P("state", None, None),
        P("state", None, None),
        P("state", None, mode),
        P(),
        P(),
        P(None, mode),
        P(),
    )
    out = P("state", mode, None)
    return jax.shard_map(
        per_device, mesh=fine, in_specs=placed, out_specs=(out, out, out), check_vma=False
    )
```

```python
import jax
import jax.numpy as jnp
from jax import lax
from jax.experimental import pallas as pl
from jax.experimental.pallas import tpu as pltpu
from jax.sharding import Mesh, PartitionSpec as P

N = 64
G = 8
PAIRS = G // 2
LANES = 2 * N
TERMS = 32
STATES = 8
SLOTS = 48
OWN_TILES = TERMS // 2
ALL_TILES = (TERMS + SLOTS) // 2
UNROLL = 4
CHUNKS = TERMS // 4
F32 = jnp.float32
BF16 = jnp.bfloat16
NT = (((1,), (1,)), ((), ()))
VMEM = pl.BlockSpec(memory_space=pltpu.VMEM)
SMEM = pl.BlockSpec(memory_space=pltpu.SMEM)
HBM = pl.BlockSpec(memory_space=pltpu.HBM)


def dot(left, right):
    return jnp.dot(left, right, preferred_element_type=F32)


def dot_nt(left, right):
    return lax.dot_general(left, right, NT, preferred_element_type=F32)


def is_left(rows):
    return lax.broadcasted_iota(jnp.int32, (rows, LANES), 1) < N


def split(value):
    high = value.astype(BF16)
    low = (value - high.astype(F32)).astype(BF16)
    return high, low


def split_lanes(value):
    return jnp.concatenate(split(value), axis=1)


def half_blocks(operator):
    left = is_left(N)
    high = operator.astype(BF16).astype(F32)
    low = operator - high
    zero = jnp.zeros_like(operator)
    return [
        jnp.where(left, high, zero).astype(BF16),
        jnp.where(left, zero, high).astype(BF16),
        jnp.where(left, low, zero).astype(BF16),
        jnp.where(left, zero, low).astype(BF16),
    ]


def tile_nt(operator):
    h0, h1, l0, l1 = half_blocks(operator)
    zero = jnp.zeros((LANES, LANES), BF16)
    high = jnp.concatenate([h0, h1], axis=0)
    low = jnp.concatenate([l0, l1], axis=0)
    return jnp.concatenate(
        [jnp.concatenate([high, low], axis=0), jnp.concatenate([high, zero], axis=0)], axis=1
    )


def tile_nn(operator):
    h0, h1, l0, l1 = half_blocks(operator)
    zero = jnp.zeros((LANES, LANES), BF16)
    high = jnp.concatenate([h0, h1], axis=0)
    low = jnp.concatenate([l0, l1], axis=0)
    return jnp.concatenate(
        [jnp.concatenate([high, low], axis=1), jnp.concatenate([high, zero], axis=1)], axis=0
    )


def spread(raw_ref, out_ref):
    left = is_left(N // 2)
    for t in range(TERMS):
        start = (t // 8) * (8 * N // 2) + t % 8
        value = raw_ref[pl.ds(start, N // 2, stride=8), :]
        turned = pltpu.roll(value, N, 1)
        out_ref[t, pl.ds(0, N // 2, stride=2), :] = jnp.where(left, value, turned)
        out_ref[t, pl.ds(1, N // 2, stride=2), :] = jnp.where(left, turned, value)


def put_term(product, weights, index, high_ref, low_ref):
    value = product[:, :LANES] + product[:, LANES:]
    rows = pl.ds(pl.multiple_of(index * N, N), N)
    left = is_left(1)
    for pair in range(PAIRS):
        weight = jnp.where(left, weights[2 * pair], weights[2 * pair + 1])
        high, low = split(value[pair * N : (pair + 1) * N] * weight)
        high_ref[rows, pair * LANES : (pair + 1) * LANES] = high
        low_ref[rows, pair * LANES : (pair + 1) * LANES] = low


def put_left(operators, index, left_ref):
    high, low = split(jnp.where(is_left(N), operators[0], operators[1]))
    columns = pl.ds(pl.multiple_of(index * LANES, LANES), LANES)
    left_ref[:N, columns] = high
    left_ref[N:, columns] = low


def act_on(left_ref, high_ref, low_ref):
    both = dot(left_ref[...], high_ref[...])
    return both[:N] + both[N:] + dot(left_ref[:N], low_ref[...])


def arrange_kernel(core_ref, raw_ref, out_ref, plain_ref, mine_ref):
    left = is_left(N // 2)
    is_first = core_ref[0] == 0
    for pair in range(PAIRS):
        one = raw_ref[pl.ds(2 * pair, N // 2, stride=G), :]
        two = raw_ref[pl.ds(2 * pair + 1, N // 2, stride=G), :]
        even = jnp.where(left, one, pltpu.roll(two, N, 1))
        odd = jnp.where(left, pltpu.roll(one, N, 1), two)
        plain_ref[pl.ds(pair * N, N // 2, stride=2), :] = even
        plain_ref[pl.ds(pair * N + 1, N // 2, stride=2), :] = odd
        mine_ref[pair * N : pair * N + N // 2, :] = jnp.where(is_first, even, odd)
        mine_ref[pair * N + N // 2 : (pair + 1) * N, :] = jnp.where(is_first, odd, even)
    for q in range(STATES):
        out_ref[q] = plain_ref[...]


def own_kernel(v_ref, cv_ref, a_ref, ap_ref, h3_ref, h2_ref, c3_ref,
               act_ref, field_ref, zh_hbm, zl_hbm,
               ops_ref, left_ref, wh_ref, wl_ref, zh_ref, zl_ref, sems):
    def chunk_copies(j):
        rows = pl.ds(pl.multiple_of(j * UNROLL * N, UNROLL * N), UNROLL * N)
        return [
            pltpu.make_async_copy(zh_ref.at[rows, :], zh_hbm.at[rows, :], sems.at[0, j]),
            pltpu.make_async_copy(zl_ref.at[rows, :], zl_hbm.at[rows, :], sems.at[1, j]),
        ]

    left_p = split_lanes(ap_ref[...])
    spread(c3_ref, ops_ref)

    def coupling_terms(j, carry):
        for u in range(UNROLL):
            k = j * UNROLL + u
            product = dot(left_p, tile_nn(ops_ref[k]))
            put_term(product, [cv_ref[k, g] for g in range(G)], k, zh_ref, zl_ref)

        @pl.when(j > 0)
        def _():
            for copy in chunk_copies(j - 1):
                copy.start()

        return carry

    lax.fori_loop(0, CHUNKS, coupling_terms, 0)

    spread(h2_ref, ops_ref)
    for i in range(OWN_TILES):
        put_left((ops_ref[2 * i], ops_ref[2 * i + 1]), i, left_ref)
    for copy in chunk_copies(CHUNKS - 1):
        copy.start()
    spread(h3_ref, ops_ref)
    left = split_lanes(a_ref[...])

    def own_terms(j, carry):
        for u in range(UNROLL):
            t = j * UNROLL + u
            product = dot_nt(left, tile_nt(ops_ref[t]))
            put_term(product, [v_ref[t, g] for g in range(G)], t, wh_ref, wl_ref)
        return carry

    lax.fori_loop(0, CHUNKS, own_terms, 0)
    act_ref[...] = act_on(left_ref, wh_ref, wl_ref)

    wide = jnp.concatenate([ap_ref[p * N : (p + 1) * N, :] for p in range(PAIRS)], axis=1)
    high, low = split(wide)
    rows_both = jnp.concatenate([high, low], axis=0)
    for j in range(CHUNKS):
        part = slice(j * UNROLL * N, (j + 1) * UNROLL * N)
        both = dot_nt(rows_both, wh_ref[part, :])
        field_ref[:, part] = both[:N] + both[N:] + dot_nt(high, wl_ref[part, :])

    for j in range(CHUNKS):
        for copy in chunk_copies(j):
            copy.wait()


def field_kernel(source_ref, term_ref, valid_ref, all_ref, own_ref, zh_hbm, zl_hbm,
                 mine_ref, other_ref, gh_ref, gl_ref, zh_ref, zl_ref, f_ref, sems):
    def chunk_copies(j):
        rows = pl.ds(pl.multiple_of(j * UNROLL * N, UNROLL * N), UNROLL * N)
        return [
            pltpu.make_async_copy(zh_hbm.at[rows, :], zh_ref.at[rows, :], sems.at[0, j]),
            pltpu.make_async_copy(zl_hbm.at[rows, :], zl_ref.at[rows, :], sems.at[1, j]),
        ]

    for j in range(CHUNKS):
        for copy in chunk_copies(j):
            copy.start()
    for q in range(STATES):
        for pair in range(PAIRS):
            high, low = split(all_ref[q, pair * N : (pair + 1) * N, :])
            lanes = slice(pair * LANES, (pair + 1) * LANES)
            gh_ref[q * N : (q + 1) * N, lanes] = high
            gl_ref[q * N : (q + 1) * N, lanes] = low
    for i in range(OWN_TILES):
        where_to = pl.ds(i, N // 2, stride=ALL_TILES)
        lanes = slice(i * LANES, (i + 1) * LANES)
        mine_ref[where_to, :] = own_ref[: N // 2, lanes]
        other_ref[where_to, :] = own_ref[N // 2 :, lanes]

    def block(j, carry):
        for copy in chunk_copies(j):
            copy.wait()
        rows = pl.ds(pl.multiple_of(j * UNROLL * N, UNROLL * N), UNROLL * N)
        zh = zh_ref[rows, :]
        left = jnp.concatenate([zh, zl_ref[rows, :], zh], axis=1)
        for half in range(2):
            here = slice(half * 4 * N, (half + 1) * 4 * N)
            gh = gh_ref[here, :]
            right = jnp.concatenate([gh, gh, gl_ref[here, :]], axis=1)
            product = dot_nt(left, right)
            f_ref[2 * half, rows, :] = product[:, :LANES]
            f_ref[2 * half + 1, rows, :] = product[:, LANES:]
        return carry

    lax.fori_loop(0, CHUNKS, block, 0)
    left_lanes = is_left(N)

    def pick(slot):
        source = source_ref[slot]
        rows = pl.ds(pl.multiple_of(term_ref[slot] * N, N), N)
        return f_ref[source // 2, rows, :], lax.rem(source, 2)

    def slot_pair(i):
        first, odd_first = pick(2 * i)
        second, odd_second = pick(2 * i + 1)
        first = jnp.where(odd_first == 1, pltpu.roll(first, N, 1), first)
        second = jnp.where(odd_second == 0, pltpu.roll(second, N, 1), second)
        first = jnp.where(valid_ref[2 * i] == 1, first, 0.0)
        second = jnp.where(valid_ref[2 * i + 1] == 1, second, 0.0)
        field = jnp.where(left_lanes, first, second)
        where_to = pl.ds(OWN_TILES + i, N // 2, stride=ALL_TILES)
        mine_ref[where_to, :] = field[: N // 2]
        other_ref[where_to, :] = field[N // 2 :]

    def slot_pairs(i, carry):
        for u in range(4):
            slot_pair(4 * i + u)
        return carry

    lax.fori_loop(0, SLOTS // 8, slot_pairs, 0)


def pair_kernel(source_ref, term_ref, valid_ref, cv_ref, all_ref, c3_ref, c2_ref, act_ref,
                out_ref, left_all_ref, ops_ref, left_ref, wh_ref, wl_ref, sum_ref):
    for q in range(STATES):
        left_all_ref[q] = split_lanes(all_ref[q])
    spread(c2_ref, ops_ref)

    def left_tiles(i, carry):
        for u in range(2):
            tile = 2 * i + u
            first, second = term_ref[2 * tile], term_ref[2 * tile + 1]
            put_left((ops_ref[first], ops_ref[second]), tile, left_ref)
        return carry

    lax.fori_loop(0, SLOTS // 4, left_tiles, 0)
    spread(c3_ref, ops_ref)

    def slot_terms(j, carry):
        for u in range(UNROLL):
            slot = j * UNROLL + u
            k = term_ref[slot]
            product = dot_nt(left_all_ref[source_ref[slot]], tile_nt(ops_ref[k]))
            is_valid = valid_ref[slot] == 1
            weights = [jnp.where(is_valid, cv_ref[k, g], 0.0) for g in range(G)]
            put_term(product, weights, slot, wh_ref, wl_ref)
        return carry

    lax.fori_loop(0, SLOTS // UNROLL, slot_terms, 0)
    action = act_ref[...] + act_on(left_ref, wh_ref, wl_ref)
    left = is_left(N // 2)
    for pair in range(PAIRS):
        sum_ref[pair * N : (pair + 1) * N, :] = action[:, pair * LANES : (pair + 1) * LANES]
        even = sum_ref[pl.ds(pair * N, N // 2, stride=2), :]
        odd = sum_ref[pl.ds(pair * N + 1, N // 2, stride=2), :]
        one = jnp.where(left, even, pltpu.roll(odd, N, 1))
        two = jnp.where(left, pltpu.roll(even, N, 1), odd)
        out_ref[pl.ds(2 * pair, N // 2, stride=G), :] = one
        out_ref[pl.ds(2 * pair + 1, N // 2, stride=G), :] = two


def total_kernel(parts_ref, own_ref, pair_ref):
    total = parts_ref[0]
    for i in range(1, N // 2):
        total = total + parts_ref[i]
    own_ref[...] = total[:OWN_TILES]
    pair_ref[...] = total[OWN_TILES:]


def shape(*dims, dtype=F32):
    return jax.ShapeDtypeStruct(dims, dtype)


def cost(flops, nbytes):
    return pl.CostEstimate(flops=flops, bytes_accessed=nbytes, transcendentals=0)


def params(mib):
    return pltpu.CompilerParams(vmem_limit_bytes=mib << 20)


OWN_GRANT = 52
FIELD_GRANT = 50


def arrange(core, raw):
    return pl.pallas_call(
        arrange_kernel,
        out_shape=(shape(STATES, PAIRS * N, LANES), shape(PAIRS * N, LANES), shape(PAIRS * N, LANES)),
        in_specs=[SMEM, VMEM],
        out_specs=[pl.BlockSpec(), VMEM, VMEM],
        compiler_params=params(8),
        name="arrange",
    )(core, raw)


def own_part(v, cv, a2, a2p, h3, h2, c3):
    big = pltpu.VMEM((TERMS * N, G * N), BF16)
    return pl.pallas_call(
        own_kernel,
        out_shape=(
            shape(N, G * N),
            shape(N, TERMS * N),
            shape(TERMS * N, G * N, dtype=BF16),
            shape(TERMS * N, G * N, dtype=BF16),
        ),
        in_specs=[SMEM] * 2 + [VMEM] * 5,
        out_specs=[VMEM] * 2 + [HBM] * 2,
        scratch_shapes=[
            pltpu.VMEM((TERMS, N, LANES), F32),
            pltpu.VMEM((LANES, TERMS * N), BF16),
            big, big, big, big,
            pltpu.SemaphoreType.DMA((2, CHUNKS)),
        ],
        compiler_params=params(OWN_GRANT),
        cost_estimate=cost(3_000_000_000, 8 << 20),
        name="own_part",
    )(v, cv, a2, a2p, h3, h2, c3)


def both_fields(source, term, valid, everyone, own, zh, zl):
    big = pltpu.VMEM((TERMS * N, G * N), BF16)
    rows = N // 2 * ALL_TILES
    return pl.pallas_call(
        field_kernel,
        out_shape=(shape(rows, LANES), shape(rows, LANES)),
        in_specs=[SMEM] * 3 + [VMEM] * 2 + [HBM] * 2,
        out_specs=[VMEM] * 2,
        scratch_shapes=[
            pltpu.VMEM((STATES * N, G * N), BF16),
            pltpu.VMEM((STATES * N, G * N), BF16),
            big, big,
            pltpu.VMEM((STATES // 2, TERMS * N, LANES), F32),
            pltpu.SemaphoreType.DMA((2, CHUNKS)),
        ],
        compiler_params=params(FIELD_GRANT),
        cost_estimate=cost(3_000_000_000, 6 << 20),
        name="both_fields",
    )(source, term, valid, everyone, own, zh, zl)


def pair_action(source, term, valid, cv, everyone, c3, c2, act):
    return pl.pallas_call(
        pair_kernel,
        out_shape=shape(PAIRS * N, LANES),
        in_specs=[SMEM] * 4 + [VMEM] * 4,
        out_specs=pl.BlockSpec(),
        scratch_shapes=[
            pltpu.VMEM((STATES, PAIRS * N, 2 * LANES), BF16),
            pltpu.VMEM((TERMS, N, LANES), F32),
            pltpu.VMEM((LANES, SLOTS * N), BF16),
            pltpu.VMEM((SLOTS * N, G * N), BF16),
            pltpu.VMEM((SLOTS * N, G * N), BF16),
            pltpu.VMEM((PAIRS * N, LANES), F32),
        ],
        compiler_params=params(24),
        cost_estimate=cost(3_000_000_000, 4 << 20),
        name="pair_action",
    )(source, term, valid, cv, everyone, c3, c2, act)


def total(parts):
    return pl.pallas_call(
        total_kernel,
        out_shape=(shape(OWN_TILES, LANES), shape(SLOTS // 2, LANES)),
        in_specs=[pl.BlockSpec()],
        out_specs=(pl.BlockSpec(), pl.BlockSpec()),
        compiler_params=params(8),
        name="total",
    )(parts)


def tile_rows(flat):
    blocks = flat.shape[0] // 8
    tiles = flat.reshape(blocks, 8, N // 2, LANES)
    return tiles.transpose(0, 2, 1, 3).reshape(blocks * 8 * N // 2, LANES)


def read_list(pairs, myself):
    is_mine = pairs[:, 0] == myself
    rank = jnp.cumsum(is_mine.astype(jnp.int32)) - 1
    slots = jnp.arange(SLOTS, dtype=jnp.int32)
    picked = (rank[None, :] == slots[:, None]) & is_mine[None, :]
    source = jnp.sum(jnp.where(picked, pairs[None, :, 1], 0), axis=1)
    term = jnp.sum(jnp.where(picked, pairs[None, :, 2], 0), axis=1)
    valid = jnp.sum(picked.astype(jnp.int32), axis=1)
    return source, term, valid


def per_device(coeffs, diag_h2, diag_h3, diag_v1, coup_h2, coup_h3, coup_v1, pairs):
    core = lax.axis_index("core").astype(jnp.int32)[None]
    to_all, plain, mine_first = arrange(core, tile_rows(coeffs[0]))
    everyone = lax.all_to_all(to_all, "state", 0, 0, tiled=True)
    listed = read_list(pairs, lax.axis_index("state"))
    c3 = tile_rows(coup_h3)
    act, own, zh, zl = own_part(
        diag_v1[0], coup_v1, plain, mine_first, tile_rows(diag_h3[0]), tile_rows(diag_h2[0]), c3
    )
    mine, other = both_fields(*listed, everyone, own, zh, zl)
    sums = mine + lax.ppermute(other, "core", [(0, 1), (1, 0)])
    parts = lax.all_to_all(
        sums.reshape(N // 2, ALL_TILES, LANES), ("z", "x"), 0, 0, tiled=True
    )
    out = pair_action(*listed, coup_v1, everyone, c3, tile_rows(coup_h2), act)
    action = out.reshape(N // 2, G, LANES).transpose(1, 0, 2).reshape(1, G, N * N)
    own_row, pair_row = total(parts)
    return action, own_row.reshape(1, 1, TERMS * N), pair_row.reshape(1, 1, SLOTS * N)


def solution(mesh):
    fine = Mesh(mesh.devices.reshape(8, 8, 4, 2), ("state", "z", "x", "core"))
    mode = ("z", "x", "core")
    placed = (
        P("state", mode, None),
        P("state", None, None),
        P("state", None, None),
        P("state", None, mode),
        P(),
        P(),
        P(None, mode),
        P(),
    )
    out = P("state", mode, None)
    return jax.shard_map(
        per_device, mesh=fine, in_specs=placed, out_specs=(out, out, out), check_vma=False
    )
```

```python
import jax
import jax.numpy as jnp
from jax import lax
from jax.experimental import pallas as pl
from jax.experimental.pallas import tpu as pltpu
from jax.sharding import Mesh, PartitionSpec as P

N = 64
G = 8
PAIRS = G // 2
LANES = 2 * N
TERMS = 32
STATES = 8
SLOTS = 48
OWN_TILES = TERMS // 2
PAIR_TILES = SLOTS // 2
X_CHIPS = 4
LAST_TILES = OWN_TILES // X_CHIPS
ALL_TILES = PAIR_TILES + LAST_TILES
UNROLL = 4
CHUNKS = TERMS // 4
F32 = jnp.float32
BF16 = jnp.bfloat16
NT = (((1,), (1,)), ((), ()))
VMEM = pl.BlockSpec(memory_space=pltpu.VMEM)
SMEM = pl.BlockSpec(memory_space=pltpu.SMEM)
HBM = pl.BlockSpec(memory_space=pltpu.HBM)


def dot(left, right):
    return jnp.dot(left, right, preferred_element_type=F32)


def dot_nt(left, right):
    return lax.dot_general(left, right, NT, preferred_element_type=F32)


def is_left(rows):
    return lax.broadcasted_iota(jnp.int32, (rows, LANES), 1) < N


def split(value):
    high = value.astype(BF16)
    low = (value - high.astype(F32)).astype(BF16)
    return high, low


def split_lanes(value):
    return jnp.concatenate(split(value), axis=1)


def half_blocks(operator):
    left = is_left(N)
    high = operator.astype(BF16).astype(F32)
    low = operator - high
    zero = jnp.zeros_like(operator)
    return [
        jnp.where(left, high, zero).astype(BF16),
        jnp.where(left, zero, high).astype(BF16),
        jnp.where(left, low, zero).astype(BF16),
        jnp.where(left, zero, low).astype(BF16),
    ]


def tile_nt(operator):
    h0, h1, l0, l1 = half_blocks(operator)
    zero = jnp.zeros((LANES, LANES), BF16)
    high = jnp.concatenate([h0, h1], axis=0)
    low = jnp.concatenate([l0, l1], axis=0)
    return jnp.concatenate(
        [jnp.concatenate([high, low], axis=0), jnp.concatenate([high, zero], axis=0)], axis=1
    )


def tile_nn(operator):
    h0, h1, l0, l1 = half_blocks(operator)
    zero = jnp.zeros((LANES, LANES), BF16)
    high = jnp.concatenate([h0, h1], axis=0)
    low = jnp.concatenate([l0, l1], axis=0)
    return jnp.concatenate(
        [jnp.concatenate([high, low], axis=1), jnp.concatenate([high, zero], axis=1)], axis=0
    )


def spread(raw_ref, out_ref):
    left = is_left(N // 2)
    for t in range(TERMS):
        start = (t // 8) * (8 * N // 2) + t % 8
        value = raw_ref[pl.ds(start, N // 2, stride=8), :]
        turned = pltpu.roll(value, N, 1)
        out_ref[t, pl.ds(0, N // 2, stride=2), :] = jnp.where(left, value, turned)
        out_ref[t, pl.ds(1, N // 2, stride=2), :] = jnp.where(left, turned, value)


def put_term(product, weights, index, high_ref, low_ref):
    value = product[:, :LANES] + product[:, LANES:]
    rows = pl.ds(pl.multiple_of(index * N, N), N)
    left = is_left(1)
    for pair in range(PAIRS):
        weight = jnp.where(left, weights[2 * pair], weights[2 * pair + 1])
        high, low = split(value[pair * N : (pair + 1) * N] * weight)
        high_ref[rows, pair * LANES : (pair + 1) * LANES] = high
        low_ref[rows, pair * LANES : (pair + 1) * LANES] = low


def put_left(operators, index, left_ref):
    high, low = split(jnp.where(is_left(N), operators[0], operators[1]))
    columns = pl.ds(pl.multiple_of(index * LANES, LANES), LANES)
    left_ref[:N, columns] = high
    left_ref[N:, columns] = low


def act_on(left_ref, high_ref, low_ref):
    both = dot(left_ref[...], high_ref[...])
    return both[:N] + both[N:] + dot(left_ref[:N], low_ref[...])


def arrange_kernel(core_ref, raw_ref, out_ref, plain_ref, mine_ref):
    left = is_left(N // 2)
    is_first = core_ref[0] == 0
    for pair in range(PAIRS):
        one = raw_ref[pl.ds(2 * pair, N // 2, stride=G), :]
        two = raw_ref[pl.ds(2 * pair + 1, N // 2, stride=G), :]
        even = jnp.where(left, one, pltpu.roll(two, N, 1))
        odd = jnp.where(left, pltpu.roll(one, N, 1), two)
        plain_ref[pl.ds(pair * N, N // 2, stride=2), :] = even
        plain_ref[pl.ds(pair * N + 1, N // 2, stride=2), :] = odd
        mine_ref[pair * N : pair * N + N // 2, :] = jnp.where(is_first, even, odd)
        mine_ref[pair * N + N // 2 : (pair + 1) * N, :] = jnp.where(is_first, odd, even)
    for q in range(STATES):
        out_ref[q] = plain_ref[...]


def own_kernel(v_ref, cv_ref, a_ref, ap_ref, h3_ref, h2_ref, c3_ref,
               act_ref, mine_ref, other_ref, zh_hbm, zl_hbm,
               ops_ref, left_ref, wh_ref, wl_ref, zh_ref, zl_ref, sems):
    def chunk_copies(j):
        rows = pl.ds(pl.multiple_of(j * UNROLL * N, UNROLL * N), UNROLL * N)
        return [
            pltpu.make_async_copy(zh_ref.at[rows, :], zh_hbm.at[rows, :], sems.at[0, j]),
            pltpu.make_async_copy(zl_ref.at[rows, :], zl_hbm.at[rows, :], sems.at[1, j]),
        ]

    left_p = split_lanes(ap_ref[...])
    spread(c3_ref, ops_ref)

    def coupling_terms(j, carry):
        for u in range(UNROLL):
            k = j * UNROLL + u
            product = dot(left_p, tile_nn(ops_ref[k]))
            put_term(product, [cv_ref[k, g] for g in range(G)], k, zh_ref, zl_ref)

        @pl.when(j > 0)
        def _():
            for copy in chunk_copies(j - 1):
                copy.start()

        return carry

    lax.fori_loop(0, CHUNKS, coupling_terms, 0)

    spread(h2_ref, ops_ref)
    for i in range(OWN_TILES):
        put_left((ops_ref[2 * i], ops_ref[2 * i + 1]), i, left_ref)
    for copy in chunk_copies(CHUNKS - 1):
        copy.start()
    spread(h3_ref, ops_ref)
    left = split_lanes(a_ref[...])

    def own_terms(j, carry):
        for u in range(UNROLL):
            t = j * UNROLL + u
            product = dot_nt(left, tile_nt(ops_ref[t]))
            put_term(product, [v_ref[t, g] for g in range(G)], t, wh_ref, wl_ref)
        return carry

    lax.fori_loop(0, CHUNKS, own_terms, 0)
    act_ref[...] = act_on(left_ref, wh_ref, wl_ref)

    wide = jnp.concatenate([ap_ref[p * N : (p + 1) * N, :] for p in range(PAIRS)], axis=1)
    high, low = split(wide)
    rows_both = jnp.concatenate([high, low], axis=0)
    for j in range(CHUNKS):
        part = slice(j * UNROLL * N, (j + 1) * UNROLL * N)
        both = dot_nt(rows_both, wh_ref[part, :])
        field = both[:N] + both[N:] + dot_nt(high, wl_ref[part, :])
        for half in range(2):
            lanes = slice(half * LANES, (half + 1) * LANES)
            rows = slice((2 * j + half) * N // 2, (2 * j + half + 1) * N // 2)
            mine_ref[rows, :] = field[: N // 2, lanes]
            other_ref[rows, :] = field[N // 2 :, lanes]

    for j in range(CHUNKS):
        for copy in chunk_copies(j):
            copy.wait()


def field_kernel(source_ref, term_ref, valid_ref, all_ref, zh_hbm, zl_hbm,
                 mine_ref, other_ref, gh_ref, gl_ref, zh_ref, zl_ref, f_ref, sems):
    def chunk_copies(j):
        rows = pl.ds(pl.multiple_of(j * UNROLL * N, UNROLL * N), UNROLL * N)
        return [
            pltpu.make_async_copy(zh_hbm.at[rows, :], zh_ref.at[rows, :], sems.at[0, j]),
            pltpu.make_async_copy(zl_hbm.at[rows, :], zl_ref.at[rows, :], sems.at[1, j]),
        ]

    for j in range(CHUNKS):
        for copy in chunk_copies(j):
            copy.start()
    for q in range(STATES):
        for pair in range(PAIRS):
            high, low = split(all_ref[q, pair * N : (pair + 1) * N, :])
            lanes = slice(pair * LANES, (pair + 1) * LANES)
            gh_ref[q * N : (q + 1) * N, lanes] = high
            gl_ref[q * N : (q + 1) * N, lanes] = low
    def block(j, carry):
        for copy in chunk_copies(2 * j) + chunk_copies(2 * j + 1):
            copy.wait()
        rows = pl.ds(pl.multiple_of(j * 2 * UNROLL * N, 2 * UNROLL * N), 2 * UNROLL * N)
        zh = zh_ref[rows, :]
        left = jnp.concatenate([zh, zl_ref[rows, :], zh], axis=1)
        for half in range(2):
            here = slice(half * 4 * N, (half + 1) * 4 * N)
            gh = gh_ref[here, :]
            right = jnp.concatenate([gh, gh, gl_ref[here, :]], axis=1)
            product = dot_nt(left, right)
            f_ref[2 * half, rows, :] = product[:, :LANES]
            f_ref[2 * half + 1, rows, :] = product[:, LANES:]
        return carry

    lax.fori_loop(0, CHUNKS // 2, block, 0)
    left_lanes = is_left(N)

    def pick(slot):
        source = source_ref[slot]
        rows = pl.ds(pl.multiple_of(term_ref[slot] * N, N), N)
        return f_ref[source // 2, rows, :], lax.rem(source, 2)

    def slot_pair(i):
        first, odd_first = pick(2 * i)
        second, odd_second = pick(2 * i + 1)
        first = jnp.where(odd_first == 1, pltpu.roll(first, N, 1), first)
        second = jnp.where(odd_second == 0, pltpu.roll(second, N, 1), second)
        first = jnp.where(valid_ref[2 * i] == 1, first, 0.0)
        second = jnp.where(valid_ref[2 * i + 1] == 1, second, 0.0)
        field = jnp.where(left_lanes, first, second)
        where_to = pl.ds(i, N // 2, stride=PAIR_TILES)
        mine_ref[where_to, :] = field[: N // 2]
        other_ref[where_to, :] = field[N // 2 :]

    def slot_pairs(i, carry):
        for u in range(8):
            slot_pair(8 * i + u)
        return carry

    lax.fori_loop(0, PAIR_TILES // 8, slot_pairs, 0)


def pair_kernel(source_ref, term_ref, valid_ref, cv_ref, all_ref, c3_ref, c2_ref, act_ref,
                out_ref, left_all_ref, ops_ref, left_ref, wh_ref, wl_ref, sum_ref):
    for q in range(STATES):
        left_all_ref[q] = split_lanes(all_ref[q])
    spread(c2_ref, ops_ref)

    def left_tiles(i, carry):
        for u in range(2):
            tile = 2 * i + u
            first, second = term_ref[2 * tile], term_ref[2 * tile + 1]
            put_left((ops_ref[first], ops_ref[second]), tile, left_ref)
        return carry

    lax.fori_loop(0, SLOTS // 4, left_tiles, 0)
    spread(c3_ref, ops_ref)

    def slot_terms(j, carry):
        for u in range(UNROLL):
            slot = j * UNROLL + u
            k = term_ref[slot]
            product = dot_nt(left_all_ref[source_ref[slot]], tile_nt(ops_ref[k]))
            is_valid = valid_ref[slot] == 1
            weights = [jnp.where(is_valid, cv_ref[k, g], 0.0) for g in range(G)]
            put_term(product, weights, slot, wh_ref, wl_ref)
        return carry

    lax.fori_loop(0, SLOTS // UNROLL, slot_terms, 0)
    action = act_ref[...] + act_on(left_ref, wh_ref, wl_ref)
    left = is_left(N // 2)
    for pair in range(PAIRS):
        sum_ref[pair * N : (pair + 1) * N, :] = action[:, pair * LANES : (pair + 1) * LANES]
        even = sum_ref[pl.ds(pair * N, N // 2, stride=2), :]
        odd = sum_ref[pl.ds(pair * N + 1, N // 2, stride=2), :]
        one = jnp.where(left, even, pltpu.roll(odd, N, 1))
        two = jnp.where(left, pltpu.roll(even, N, 1), odd)
        out_ref[pl.ds(2 * pair, N // 2, stride=G), :] = one
        out_ref[pl.ds(2 * pair + 1, N // 2, stride=G), :] = two


def merge_kernel(mine_ref, theirs_ref, own_ref, out_ref):
    for a in range(N // 2):
        here = slice(a * PAIR_TILES, (a + 1) * PAIR_TILES)
        out_ref[a * ALL_TILES : a * ALL_TILES + PAIR_TILES, :] = mine_ref[here, :] + theirs_ref[here, :]
    for r in range(LAST_TILES):
        out_ref[pl.ds(PAIR_TILES + r, N // 2, stride=ALL_TILES), :] = own_ref[r]


def total_kernel(parts_ref, own_ref, pair_ref):
    def part(i, first, count):
        return parts_ref[i * ALL_TILES + first : i * ALL_TILES + first + count, :]

    total = part(0, 0, PAIR_TILES)
    for i in range(1, N // 2):
        total = total + part(i, 0, PAIR_TILES)
    pair_ref[...] = total
    for x in range(X_CHIPS):
        total = part(x, PAIR_TILES, LAST_TILES)
        for z in range(1, N // 2 // X_CHIPS):
            total = total + part(z * X_CHIPS + x, PAIR_TILES, LAST_TILES)
        own_ref[x * LAST_TILES : (x + 1) * LAST_TILES, :] = total


def shape(*dims, dtype=F32):
    return jax.ShapeDtypeStruct(dims, dtype)


def cost(flops, nbytes):
    return pl.CostEstimate(flops=flops, bytes_accessed=nbytes, transcendentals=0)


def params(mib):
    return pltpu.CompilerParams(vmem_limit_bytes=mib << 20)


OWN_GRANT = 52
FIELD_GRANT = 52


def arrange(core, raw):
    return pl.pallas_call(
        arrange_kernel,
        out_shape=(shape(STATES, PAIRS * N, LANES), shape(PAIRS * N, LANES), shape(PAIRS * N, LANES)),
        in_specs=[SMEM, VMEM],
        out_specs=[pl.BlockSpec(), VMEM, VMEM],
        compiler_params=params(8),
        name="arrange",
    )(core, raw)


def own_part(v, cv, a2, a2p, h3, h2, c3):
    big = pltpu.VMEM((TERMS * N, G * N), BF16)
    return pl.pallas_call(
        own_kernel,
        out_shape=(
            shape(N, G * N),
            shape(N // 2 * OWN_TILES, LANES),
            shape(N // 2 * OWN_TILES, LANES),
            shape(TERMS * N, G * N, dtype=BF16),
            shape(TERMS * N, G * N, dtype=BF16),
        ),
        in_specs=[SMEM] * 2 + [VMEM] * 5,
        out_specs=[VMEM] * 3 + [HBM] * 2,
        scratch_shapes=[
            pltpu.VMEM((TERMS, N, LANES), F32),
            pltpu.VMEM((LANES, TERMS * N), BF16),
            big, big, big, big,
            pltpu.SemaphoreType.DMA((2, CHUNKS)),
        ],
        compiler_params=params(OWN_GRANT),
        cost_estimate=cost(3_000_000_000, 8 << 20),
        name="own_part",
    )(v, cv, a2, a2p, h3, h2, c3)


def pair_fields(source, term, valid, everyone, zh, zl):
    big = pltpu.VMEM((TERMS * N, G * N), BF16)
    rows = N // 2 * PAIR_TILES
    return pl.pallas_call(
        field_kernel,
        out_shape=(shape(rows, LANES), shape(rows, LANES)),
        in_specs=[SMEM] * 3 + [VMEM] + [HBM] * 2,
        out_specs=[VMEM] * 2,
        scratch_shapes=[
            pltpu.VMEM((STATES * N, G * N), BF16),
            pltpu.VMEM((STATES * N, G * N), BF16),
            big, big,
            pltpu.VMEM((STATES // 2, TERMS * N, LANES), F32),
            pltpu.SemaphoreType.DMA((2, CHUNKS)),
        ],
        compiler_params=params(FIELD_GRANT),
        cost_estimate=cost(3_000_000_000, 6 << 20),
        name="pair_fields",
    )(source, term, valid, everyone, zh, zl)


def pair_action(source, term, valid, cv, everyone, c3, c2, act):
    return pl.pallas_call(
        pair_kernel,
        out_shape=shape(PAIRS * N, LANES),
        in_specs=[SMEM] * 4 + [VMEM] * 4,
        out_specs=pl.BlockSpec(),
        scratch_shapes=[
            pltpu.VMEM((STATES, PAIRS * N, 2 * LANES), BF16),
            pltpu.VMEM((TERMS, N, LANES), F32),
            pltpu.VMEM((LANES, SLOTS * N), BF16),
            pltpu.VMEM((SLOTS * N, G * N), BF16),
            pltpu.VMEM((SLOTS * N, G * N), BF16),
            pltpu.VMEM((PAIRS * N, LANES), F32),
        ],
        compiler_params=params(24),
        cost_estimate=cost(3_000_000_000, 4 << 20),
        name="pair_action",
    )(source, term, valid, cv, everyone, c3, c2, act)


def merge(mine, theirs, own):
    return pl.pallas_call(
        merge_kernel,
        out_shape=shape(N // 2 * ALL_TILES, LANES),
        in_specs=[VMEM] * 3,
        out_specs=pl.BlockSpec(),
        compiler_params=params(8),
        name="merge",
    )(mine, theirs, own)


def total(parts):
    return pl.pallas_call(
        total_kernel,
        out_shape=(shape(OWN_TILES, LANES), shape(PAIR_TILES, LANES)),
        in_specs=[pl.BlockSpec()],
        out_specs=(pl.BlockSpec(), pl.BlockSpec()),
        compiler_params=params(8),
        name="total",
    )(parts)


def tile_rows(flat):
    blocks = flat.shape[0] // 8
    tiles = flat.reshape(blocks, 8, N // 2, LANES)
    return tiles.transpose(0, 2, 1, 3).reshape(blocks * 8 * N // 2, LANES)


def read_list(pairs, myself):
    is_mine = pairs[:, 0] == myself
    rank = jnp.cumsum(is_mine.astype(jnp.int32)) - 1
    slots = jnp.arange(SLOTS, dtype=jnp.int32)
    picked = (rank[None, :] == slots[:, None]) & is_mine[None, :]
    source = jnp.sum(jnp.where(picked, pairs[None, :, 1], 0), axis=1)
    term = jnp.sum(jnp.where(picked, pairs[None, :, 2], 0), axis=1)
    valid = jnp.sum(picked.astype(jnp.int32), axis=1)
    return source, term, valid


def other_core(value):
    return lax.ppermute(value, "core", [(0, 1), (1, 0)])


def reduce_own(mine, other):
    x = lax.axis_index("x")
    tiles = (mine + other_core(other)).reshape(2, 2, LAST_TILES, N // 2, LANES)
    for axis, bit in ((1, 1), (0, 2)):
        mine_here = (x // bit) % 2
        keep = lax.dynamic_index_in_dim(tiles, mine_here, axis, False)
        send = lax.dynamic_index_in_dim(tiles, 1 - mine_here, axis, False)
        tiles = keep + lax.ppermute(send, "x", [(i, i ^ bit) for i in range(X_CHIPS)])
    return tiles


def per_device(coeffs, diag_h2, diag_h3, diag_v1, coup_h2, coup_h3, coup_v1, pairs):
    core = lax.axis_index("core").astype(jnp.int32)[None]
    to_all, plain, mine_first = arrange(core, tile_rows(coeffs[0]))
    everyone = lax.all_to_all(to_all, "state", 0, 0, tiled=True)
    listed = read_list(pairs, lax.axis_index("state"))
    c3 = tile_rows(coup_h3)
    act, own_mine, own_other, zh, zl = own_part(
        diag_v1[0], coup_v1, plain, mine_first, tile_rows(diag_h3[0]), tile_rows(diag_h2[0]), c3
    )
    everyone, own_columns = lax.optimization_barrier(
        (everyone, reduce_own(own_mine, own_other))
    )
    pair_mine, pair_other = pair_fields(*listed, everyone, zh, zl)
    sums = merge(pair_mine, other_core(pair_other), own_columns)
    parts = lax.all_to_all(
        sums.reshape(N // 2, 1, ALL_TILES * LANES), ("z", "x"), 0, 0, tiled=True
    )
    out = pair_action(*listed, coup_v1, everyone, c3, tile_rows(coup_h2), act)
    action = out.reshape(N // 2, G, LANES).transpose(1, 0, 2).reshape(1, G, N * N)
    own_row, pair_row = total(parts.reshape(N // 2 * ALL_TILES, LANES))
    return action, own_row.reshape(1, 1, TERMS * N), pair_row.reshape(1, 1, SLOTS * N)


def solution(mesh):
    fine = Mesh(mesh.devices.reshape(8, 8, 4, 2), ("state", "z", "x", "core"))
    mode = ("z", "x", "core")
    placed = (
        P("state", mode, None),
        P("state", None, None),
        P("state", None, None),
        P("state", None, mode),
        P(),
        P(),
        P(None, mode),
        P(),
    )
    out = P("state", mode, None)
    return jax.shard_map(
        per_device, mesh=fine, in_specs=placed, out_specs=(out, out, out), check_vma=False
    )
```

```python
import functools

import jax
import jax.numpy as jnp
from jax import lax
from jax.experimental import pallas as pl
from jax.experimental.pallas import tpu as pltpu
from jax.sharding import Mesh, PartitionSpec as P

N = 64
G = 8
PAIRS = G // 2
LANES = 2 * N
TERMS = 32
STATES = 8
SLOTS = 48
OWN_TILES = TERMS // 2
PAIR_TILES = SLOTS // 2
ALL_TILES = OWN_TILES + PAIR_TILES
X_CHIPS = 4
Z_CHIPS = 8
HALF_SLOTS = SLOTS // 2
UNROLL = 4
CHUNKS = TERMS // 4
F32 = jnp.float32
BF16 = jnp.bfloat16
NT = (((1,), (1,)), ((), ()))
VMEM = pl.BlockSpec(memory_space=pltpu.VMEM)
SMEM = pl.BlockSpec(memory_space=pltpu.SMEM)
HBM = pl.BlockSpec(memory_space=pltpu.HBM)


def dot(left, right):
    return jnp.dot(left, right, preferred_element_type=F32)


def dot_nt(left, right):
    return lax.dot_general(left, right, NT, preferred_element_type=F32)


def is_left(rows):
    return lax.broadcasted_iota(jnp.int32, (rows, LANES), 1) < N


def split(value):
    high = value.astype(BF16)
    low = (value - high.astype(F32)).astype(BF16)
    return high, low


def split_lanes(value):
    return jnp.concatenate(split(value), axis=1)


def half_blocks(operator):
    left = is_left(N)
    high = operator.astype(BF16).astype(F32)
    low = operator - high
    zero = jnp.zeros_like(operator)
    return [
        jnp.where(left, high, zero).astype(BF16),
        jnp.where(left, zero, high).astype(BF16),
        jnp.where(left, low, zero).astype(BF16),
        jnp.where(left, zero, low).astype(BF16),
    ]


def tile_nt(operator):
    h0, h1, l0, l1 = half_blocks(operator)
    zero = jnp.zeros((LANES, LANES), BF16)
    high = jnp.concatenate([h0, h1], axis=0)
    low = jnp.concatenate([l0, l1], axis=0)
    return jnp.concatenate(
        [jnp.concatenate([high, low], axis=0), jnp.concatenate([high, zero], axis=0)], axis=1
    )


def tile_nn(operator):
    h0, h1, l0, l1 = half_blocks(operator)
    zero = jnp.zeros((LANES, LANES), BF16)
    high = jnp.concatenate([h0, h1], axis=0)
    low = jnp.concatenate([l0, l1], axis=0)
    return jnp.concatenate(
        [jnp.concatenate([high, low], axis=1), jnp.concatenate([high, zero], axis=1)], axis=0
    )


def spread(raw_ref, out_ref):
    left = is_left(N // 2)
    for t in range(TERMS):
        start = (t // 8) * (8 * N // 2) + t % 8
        value = raw_ref[pl.ds(start, N // 2, stride=8), :]
        turned = pltpu.roll(value, N, 1)
        out_ref[t, pl.ds(0, N // 2, stride=2), :] = jnp.where(left, value, turned)
        out_ref[t, pl.ds(1, N // 2, stride=2), :] = jnp.where(left, turned, value)


def put_term(product, weights, index, high_ref, low_ref):
    value = product[:, :LANES] + product[:, LANES:]
    rows = pl.ds(pl.multiple_of(index * N, N), N)
    left = is_left(1)
    for pair in range(PAIRS):
        weight = jnp.where(left, weights[2 * pair], weights[2 * pair + 1])
        high, low = split(value[pair * N : (pair + 1) * N] * weight)
        high_ref[rows, pair * LANES : (pair + 1) * LANES] = high
        low_ref[rows, pair * LANES : (pair + 1) * LANES] = low


def put_left(operators, index, left_ref):
    high, low = split(jnp.where(is_left(N), operators[0], operators[1]))
    columns = pl.ds(pl.multiple_of(index * LANES, LANES), LANES)
    left_ref[:N, columns] = high
    left_ref[N:, columns] = low


def act_on(left_ref, high_ref, low_ref):
    both = dot(left_ref[...], high_ref[...])
    return both[:N] + both[N:] + dot(left_ref[:N], low_ref[...])


def arrange_kernel(core_ref, raw_ref, out_ref, plain_ref, mine_ref):
    left = is_left(N // 2)
    is_first = core_ref[0] == 0
    for pair in range(PAIRS):
        one = raw_ref[pl.ds(2 * pair, N // 2, stride=G), :]
        two = raw_ref[pl.ds(2 * pair + 1, N // 2, stride=G), :]
        even = jnp.where(left, one, pltpu.roll(two, N, 1))
        odd = jnp.where(left, pltpu.roll(one, N, 1), two)
        plain_ref[pl.ds(pair * N, N // 2, stride=2), :] = even
        plain_ref[pl.ds(pair * N + 1, N // 2, stride=2), :] = odd
        for x in range(X_CHIPS):
            first = plain_ref[pl.ds(pair * N + 2 * x, Z_CHIPS, stride=2 * X_CHIPS), :]
            second = plain_ref[pl.ds(pair * N + 2 * x + 1, Z_CHIPS, stride=2 * X_CHIPS), :]
            start = pair * N + x * Z_CHIPS
            mine_ref[start : start + Z_CHIPS, :] = jnp.where(is_first, first, second)
            start += N // 2
            mine_ref[start : start + Z_CHIPS, :] = jnp.where(is_first, second, first)
    for q in range(STATES):
        out_ref[q] = plain_ref[...]


def own_kernel(v_ref, cv_ref, a_ref, ap_ref, h3_ref, h2_ref, c3_ref,
               act_ref, mine_ref, other_ref, zh_hbm, zl_hbm,
               ops_ref, left_ref, wh_ref, wl_ref, zh_ref, zl_ref, sems):
    def chunk_copies(j):
        rows = pl.ds(pl.multiple_of(j * UNROLL * N, UNROLL * N), UNROLL * N)
        return [
            pltpu.make_async_copy(zh_ref.at[rows, :], zh_hbm.at[rows, :], sems.at[0, j]),
            pltpu.make_async_copy(zl_ref.at[rows, :], zl_hbm.at[rows, :], sems.at[1, j]),
        ]

    left_p = split_lanes(ap_ref[...])
    spread(c3_ref, ops_ref)

    def coupling_terms(j, carry):
        for u in range(UNROLL):
            k = j * UNROLL + u
            product = dot(left_p, tile_nn(ops_ref[k]))
            put_term(product, [cv_ref[k, g] for g in range(G)], k, zh_ref, zl_ref)

        @pl.when(j > 0)
        def _():
            for copy in chunk_copies(j - 1):
                copy.start()

        return carry

    lax.fori_loop(0, CHUNKS, coupling_terms, 0)

    spread(h2_ref, ops_ref)
    for i in range(OWN_TILES):
        put_left((ops_ref[2 * i], ops_ref[2 * i + 1]), i, left_ref)
    for copy in chunk_copies(CHUNKS - 1):
        copy.start()
    spread(h3_ref, ops_ref)
    left = split_lanes(a_ref[...])

    def own_terms(j, carry):
        for u in range(UNROLL):
            t = j * UNROLL + u
            product = dot_nt(left, tile_nt(ops_ref[t]))
            put_term(product, [v_ref[t, g] for g in range(G)], t, wh_ref, wl_ref)
        return carry

    lax.fori_loop(0, CHUNKS, own_terms, 0)
    act_ref[...] = act_on(left_ref, wh_ref, wl_ref)

    wide = jnp.concatenate([ap_ref[p * N : (p + 1) * N, :] for p in range(PAIRS)], axis=1)
    high, low = split(wide)
    rows_both = jnp.concatenate([high, low], axis=0)
    for j in range(CHUNKS):
        part = slice(j * UNROLL * N, (j + 1) * UNROLL * N)
        both = dot_nt(rows_both, wh_ref[part, :])
        field = both[:N] + both[N:] + dot_nt(high, wl_ref[part, :])
        for half in range(2):
            lanes = slice(half * LANES, (half + 1) * LANES)
            rows = slice((2 * j + half) * N // 2, (2 * j + half + 1) * N // 2)
            mine_ref[rows, :] = field[: N // 2, lanes]
            other_ref[rows, :] = field[N // 2 :, lanes]

    for j in range(CHUNKS):
        for copy in chunk_copies(j):
            copy.wait()


def field_kernel(source_ref, term_ref, valid_ref, all_ref, zh_hbm, zl_hbm,
                 mine_ref, other_ref, gh_ref, gl_ref, zh_ref, zl_ref, f_ref, sems):
    def chunk_copies(j):
        rows = pl.ds(pl.multiple_of(j * UNROLL * N, UNROLL * N), UNROLL * N)
        return [
            pltpu.make_async_copy(zh_hbm.at[rows, :], zh_ref.at[rows, :], sems.at[0, j]),
            pltpu.make_async_copy(zl_hbm.at[rows, :], zl_ref.at[rows, :], sems.at[1, j]),
        ]

    for j in range(CHUNKS):
        for copy in chunk_copies(j):
            copy.start()
    for q in range(STATES):
        for pair in range(PAIRS):
            high, low = split(all_ref[q, pair * N : (pair + 1) * N, :])
            lanes = slice(pair * LANES, (pair + 1) * LANES)
            gh_ref[q * N : (q + 1) * N, lanes] = high
            gl_ref[q * N : (q + 1) * N, lanes] = low
    def block(j, carry):
        for copy in chunk_copies(2 * j) + chunk_copies(2 * j + 1):
            copy.wait()
        rows = pl.ds(pl.multiple_of(j * 2 * UNROLL * N, 2 * UNROLL * N), 2 * UNROLL * N)
        zh = zh_ref[rows, :]
        left = jnp.concatenate([zh, zl_ref[rows, :], zh], axis=1)
        for half in range(2):
            here = slice(half * 4 * N, (half + 1) * 4 * N)
            gh = gh_ref[here, :]
            right = jnp.concatenate([gh, gh, gl_ref[here, :]], axis=1)
            product = dot_nt(left, right)
            f_ref[2 * half, rows, :] = product[:, :LANES]
            f_ref[2 * half + 1, rows, :] = product[:, LANES:]
        return carry

    lax.fori_loop(0, CHUNKS // 2, block, 0)
    left_lanes = is_left(N)

    def pick(slot):
        source = source_ref[slot]
        rows = pl.ds(pl.multiple_of(term_ref[slot] * N, N), N)
        return f_ref[source // 2, rows, :], lax.rem(source, 2)

    def slot_pair(i):
        first, odd_first = pick(2 * i)
        second, odd_second = pick(2 * i + 1)
        first = jnp.where(odd_first == 1, pltpu.roll(first, N, 1), first)
        second = jnp.where(odd_second == 0, pltpu.roll(second, N, 1), second)
        first = jnp.where(valid_ref[2 * i] == 1, first, 0.0)
        second = jnp.where(valid_ref[2 * i + 1] == 1, second, 0.0)
        field = jnp.where(left_lanes, first, second)
        where_to = pl.ds(i, N // 2, stride=PAIR_TILES)
        mine_ref[where_to, :] = field[: N // 2]
        other_ref[where_to, :] = field[N // 2 :]

    def slot_pairs(i, carry):
        for u in range(8):
            slot_pair(8 * i + u)
        return carry

    lax.fori_loop(0, PAIR_TILES // 8, slot_pairs, 0)


def pair_kernel(base, source_ref, term_ref, valid_ref, cv_ref, all_ref, c3_ref, c2_ref, act_ref,
                out_ref, left_all_ref, ops_ref, left_ref, wh_ref, wl_ref, *sum_ref):
    for q in range(STATES):
        left_all_ref[q] = split_lanes(all_ref[q])
    spread(c2_ref, ops_ref)

    def left_tiles(i, carry):
        for u in range(2):
            tile = 2 * i + u
            first, second = term_ref[base + 2 * tile], term_ref[base + 2 * tile + 1]
            put_left((ops_ref[first], ops_ref[second]), tile, left_ref)
        return carry

    lax.fori_loop(0, HALF_SLOTS // 4, left_tiles, 0)
    spread(c3_ref, ops_ref)

    def slot_terms(j, carry):
        for u in range(UNROLL):
            slot = j * UNROLL + u
            k = term_ref[base + slot]
            product = dot_nt(left_all_ref[source_ref[base + slot]], tile_nt(ops_ref[k]))
            is_valid = valid_ref[base + slot] == 1
            weights = [jnp.where(is_valid, cv_ref[k, g], 0.0) for g in range(G)]
            put_term(product, weights, slot, wh_ref, wl_ref)
        return carry

    lax.fori_loop(0, HALF_SLOTS // UNROLL, slot_terms, 0)
    action = act_ref[...] + act_on(left_ref, wh_ref, wl_ref)
    if base == 0:
        out_ref[...] = action
        return
    (sum_ref,) = sum_ref
    left = is_left(N // 2)
    for pair in range(PAIRS):
        sum_ref[pair * N : (pair + 1) * N, :] = action[:, pair * LANES : (pair + 1) * LANES]
        even = sum_ref[pl.ds(pair * N, N // 2, stride=2), :]
        odd = sum_ref[pl.ds(pair * N + 1, N // 2, stride=2), :]
        one = jnp.where(left, even, pltpu.roll(odd, N, 1))
        two = jnp.where(left, pltpu.roll(even, N, 1), odd)
        out_ref[pl.ds(2 * pair, N // 2, stride=G), :] = one
        out_ref[pl.ds(2 * pair + 1, N // 2, stride=G), :] = two


def merge_kernel(parts_ref, own_ref, out_ref):
    for z in range(Z_CHIPS):
        total = parts_ref[0, z * PAIR_TILES : (z + 1) * PAIR_TILES, :]
        for x in range(1, X_CHIPS):
            total = total + parts_ref[x, z * PAIR_TILES : (z + 1) * PAIR_TILES, :]
        out_ref[z * ALL_TILES : z * ALL_TILES + PAIR_TILES, :] = total
    for i in range(OWN_TILES):
        out_ref[pl.ds(PAIR_TILES + i, Z_CHIPS, stride=ALL_TILES), :] = own_ref[i]


def total_kernel(parts_ref, own_ref, pair_ref):
    total = parts_ref[0]
    for z in range(1, Z_CHIPS):
        total = total + parts_ref[z]
    pair_ref[...] = total[:PAIR_TILES]
    own_ref[...] = total[PAIR_TILES:]


def shape(*dims, dtype=F32):
    return jax.ShapeDtypeStruct(dims, dtype)


def cost(flops, nbytes):
    return pl.CostEstimate(flops=flops, bytes_accessed=nbytes, transcendentals=0)


def params(mib):
    return pltpu.CompilerParams(vmem_limit_bytes=mib << 20)


OWN_GRANT = 52
FIELD_GRANT = 52


def arrange(core, raw):
    return pl.pallas_call(
        arrange_kernel,
        out_shape=(shape(STATES, PAIRS * N, LANES), shape(PAIRS * N, LANES), shape(PAIRS * N, LANES)),
        in_specs=[SMEM, VMEM],
        out_specs=[pl.BlockSpec(), VMEM, VMEM],
        compiler_params=params(8),
        name="arrange",
    )(core, raw)


def own_part(v, cv, a2, a2p, h3, h2, c3):
    big = pltpu.VMEM((TERMS * N, G * N), BF16)
    return pl.pallas_call(
        own_kernel,
        out_shape=(
            shape(N, G * N),
            shape(N // 2 * OWN_TILES, LANES),
            shape(N // 2 * OWN_TILES, LANES),
            shape(TERMS * N, G * N, dtype=BF16),
            shape(TERMS * N, G * N, dtype=BF16),
        ),
        in_specs=[SMEM] * 2 + [VMEM] * 5,
        out_specs=[VMEM] * 3 + [HBM] * 2,
        scratch_shapes=[
            pltpu.VMEM((TERMS, N, LANES), F32),
            pltpu.VMEM((LANES, TERMS * N), BF16),
            big, big, big, big,
            pltpu.SemaphoreType.DMA((2, CHUNKS)),
        ],
        compiler_params=params(OWN_GRANT),
        cost_estimate=cost(3_000_000_000, 8 << 20),
        name="own_part",
    )(v, cv, a2, a2p, h3, h2, c3)


def pair_fields(source, term, valid, everyone, zh, zl):
    big = pltpu.VMEM((TERMS * N, G * N), BF16)
    rows = N // 2 * PAIR_TILES
    return pl.pallas_call(
        field_kernel,
        out_shape=(shape(rows, LANES), shape(rows, LANES)),
        in_specs=[SMEM] * 3 + [VMEM] + [HBM] * 2,
        out_specs=[VMEM] * 2,
        scratch_shapes=[
            pltpu.VMEM((STATES * N, G * N), BF16),
            pltpu.VMEM((STATES * N, G * N), BF16),
            big, big,
            pltpu.VMEM((STATES // 2, TERMS * N, LANES), F32),
            pltpu.SemaphoreType.DMA((2, CHUNKS)),
        ],
        compiler_params=params(FIELD_GRANT),
        cost_estimate=cost(3_000_000_000, 6 << 20),
        name="pair_fields",
    )(source, term, valid, everyone, zh, zl)


def pair_action(base, source, term, valid, cv, everyone, c3, c2, act):
    last = [pltpu.VMEM((PAIRS * N, LANES), F32)] if base else []
    return pl.pallas_call(
        functools.partial(pair_kernel, base),
        out_shape=shape(PAIRS * N, LANES) if base else shape(N, G * N),
        in_specs=[SMEM] * 4 + [VMEM] * 4,
        out_specs=pl.BlockSpec() if base else VMEM,
        scratch_shapes=[
            pltpu.VMEM((STATES, PAIRS * N, 2 * LANES), BF16),
            pltpu.VMEM((TERMS, N, LANES), F32),
            pltpu.VMEM((LANES, HALF_SLOTS * N), BF16),
            pltpu.VMEM((HALF_SLOTS * N, G * N), BF16),
            pltpu.VMEM((HALF_SLOTS * N, G * N), BF16),
        ]
        + last,
        compiler_params=params(24),
        cost_estimate=cost(1_500_000_000, 4 << 20),
        name="pair_action_last" if base else "pair_action_first",
    )(source, term, valid, cv, everyone, c3, c2, act)


def merge(parts, own):
    return pl.pallas_call(
        merge_kernel,
        out_shape=shape(Z_CHIPS * ALL_TILES, LANES),
        in_specs=[VMEM] * 2,
        out_specs=pl.BlockSpec(),
        compiler_params=params(8),
        name="merge",
    )(parts, own)


def total(parts):
    return pl.pallas_call(
        total_kernel,
        out_shape=(shape(OWN_TILES, LANES), shape(PAIR_TILES, LANES)),
        in_specs=[pl.BlockSpec()],
        out_specs=(pl.BlockSpec(), pl.BlockSpec()),
        compiler_params=params(8),
        name="total",
    )(parts)


def tile_rows(flat):
    blocks = flat.shape[0] // 8
    tiles = flat.reshape(blocks, 8, N // 2, LANES)
    return tiles.transpose(0, 2, 1, 3).reshape(blocks * 8 * N // 2, LANES)


def read_list(pairs, myself):
    is_mine = pairs[:, 0] == myself
    rank = jnp.cumsum(is_mine.astype(jnp.int32)) - 1
    slots = jnp.arange(SLOTS, dtype=jnp.int32)
    picked = (rank[None, :] == slots[:, None]) & is_mine[None, :]
    source = jnp.sum(jnp.where(picked, pairs[None, :, 1], 0), axis=1)
    term = jnp.sum(jnp.where(picked, pairs[None, :, 2], 0), axis=1)
    valid = jnp.sum(picked.astype(jnp.int32), axis=1)
    return source, term, valid


def other_core(value):
    return lax.ppermute(value, "core", [(0, 1), (1, 0)])


def reduce_own(mine, other):
    x = lax.axis_index("x")
    tiles = (mine + other_core(other)).reshape(OWN_TILES, 2, 2, Z_CHIPS, LANES)
    for axis, bit in ((2, 1), (1, 2)):
        mine_here = (x // bit) % 2
        keep = lax.dynamic_index_in_dim(tiles, mine_here, axis, False)
        send = lax.dynamic_index_in_dim(tiles, 1 - mine_here, axis, False)
        tiles = keep + lax.ppermute(send, "x", [(i, i ^ bit) for i in range(X_CHIPS)])
    return tiles


def per_device(coeffs, diag_h2, diag_h3, diag_v1, coup_h2, coup_h3, coup_v1, pairs):
    core = lax.axis_index("core").astype(jnp.int32)[None]
    to_all, plain, mine_first = arrange(core, tile_rows(coeffs[0]))
    everyone = lax.all_to_all(to_all, "state", 0, 0, tiled=True)
    listed = read_list(pairs, lax.axis_index("state"))
    c3 = tile_rows(coup_h3)
    act, own_mine, own_other, zh, zl = own_part(
        diag_v1[0], coup_v1, plain, mine_first, tile_rows(diag_h3[0]), tile_rows(diag_h2[0]), c3
    )
    everyone, own_rows = lax.optimization_barrier(
        (everyone, reduce_own(own_mine, own_other))
    )
    pair_mine, pair_other = pair_fields(*listed, everyone, zh, zl)
    sums = pair_mine + other_core(pair_other)
    parts = lax.all_to_all(
        sums.reshape(X_CHIPS, Z_CHIPS * PAIR_TILES, LANES), "x", 0, 0, tiled=True
    )
    c2 = tile_rows(coup_h2)
    act = pair_action(0, *listed, coup_v1, everyone, c3, c2, act)
    act, sums = lax.optimization_barrier((act, merge(parts, own_rows)))
    parts = lax.all_to_all(sums.reshape(Z_CHIPS, ALL_TILES, LANES), "z", 0, 0, tiled=True)
    out = pair_action(HALF_SLOTS, *listed, coup_v1, everyone, c3, c2, act)
    action = out.reshape(N // 2, G, LANES).transpose(1, 0, 2).reshape(1, G, N * N)
    own_row, pair_row = total(parts)
    return action, own_row.reshape(1, 1, TERMS * N), pair_row.reshape(1, 1, SLOTS * N)


def solution(mesh):
    fine = Mesh(mesh.devices.reshape(8, 8, 4, 2), ("state", "z", "x", "core"))
    mode = ("z", "x", "core")
    placed = (
        P("state", mode, None),
        P("state", None, None),
        P("state", None, None),
        P("state", None, mode),
        P(),
        P(),
        P(None, mode),
        P(),
    )
    out = P("state", mode, None)
    return jax.shard_map(
        per_device, mesh=fine, in_specs=placed, out_specs=(out, out, out), check_vma=False
    )
```

```python
import jax
import jax.numpy as jnp
from jax import lax
from jax.experimental import pallas as pl
from jax.experimental.pallas import tpu as pltpu
from jax.sharding import Mesh, PartitionSpec as P

N = 64
G = 8
PAIRS = G // 2
LANES = 2 * N
TERMS = 32
STATES = 8
SLOTS = 48
OWN_TILES = TERMS // 2
PAIR_TILES = SLOTS // 2
X_CHIPS = 4
LAST_TILES = OWN_TILES // X_CHIPS
ALL_TILES = PAIR_TILES + LAST_TILES
UNROLL = 4
CHUNKS = TERMS // 4
F32 = jnp.float32
BF16 = jnp.bfloat16
NT = (((1,), (1,)), ((), ()))
VMEM = pl.BlockSpec(memory_space=pltpu.VMEM)
SMEM = pl.BlockSpec(memory_space=pltpu.SMEM)
HBM = pl.BlockSpec(memory_space=pltpu.HBM)


def dot(left, right):
    return jnp.dot(left, right, preferred_element_type=F32)


def dot_nt(left, right):
    return lax.dot_general(left, right, NT, preferred_element_type=F32)


def is_left(rows):
    return lax.broadcasted_iota(jnp.int32, (rows, LANES), 1) < N


def split(value):
    high = value.astype(BF16)
    low = (value - high.astype(F32)).astype(BF16)
    return high, low


def split_lanes(value):
    return jnp.concatenate(split(value), axis=1)


def half_blocks(operator):
    left = is_left(N)
    high = operator.astype(BF16).astype(F32)
    low = operator - high
    zero = jnp.zeros_like(operator)
    return [
        jnp.where(left, high, zero).astype(BF16),
        jnp.where(left, zero, high).astype(BF16),
        jnp.where(left, low, zero).astype(BF16),
        jnp.where(left, zero, low).astype(BF16),
    ]


def tile_nt(operator):
    h0, h1, l0, l1 = half_blocks(operator)
    zero = jnp.zeros((LANES, LANES), BF16)
    high = jnp.concatenate([h0, h1], axis=0)
    low = jnp.concatenate([l0, l1], axis=0)
    return jnp.concatenate(
        [jnp.concatenate([high, low], axis=0), jnp.concatenate([high, zero], axis=0)], axis=1
    )


def tile_nn(operator):
    h0, h1, l0, l1 = half_blocks(operator)
    zero = jnp.zeros((LANES, LANES), BF16)
    high = jnp.concatenate([h0, h1], axis=0)
    low = jnp.concatenate([l0, l1], axis=0)
    return jnp.concatenate(
        [jnp.concatenate([high, low], axis=1), jnp.concatenate([high, zero], axis=1)], axis=0
    )


def spread(raw_ref, out_ref):
    left = is_left(N // 2)
    for t in range(TERMS):
        start = (t // 8) * (8 * N // 2) + t % 8
        value = raw_ref[pl.ds(start, N // 2, stride=8), :]
        turned = pltpu.roll(value, N, 1)
        out_ref[t, pl.ds(0, N // 2, stride=2), :] = jnp.where(left, value, turned)
        out_ref[t, pl.ds(1, N // 2, stride=2), :] = jnp.where(left, turned, value)


def put_term(product, weights, index, high_ref, low_ref):
    value = product[:, :LANES] + product[:, LANES:]
    rows = pl.ds(pl.multiple_of(index * N, N), N)
    left = is_left(1)
    for pair in range(PAIRS):
        weight = jnp.where(left, weights[2 * pair], weights[2 * pair + 1])
        high, low = split(value[pair * N : (pair + 1) * N] * weight)
        high_ref[rows, pair * LANES : (pair + 1) * LANES] = high
        low_ref[rows, pair * LANES : (pair + 1) * LANES] = low


def put_left(operators, index, left_ref):
    high, low = split(jnp.where(is_left(N), operators[0], operators[1]))
    columns = pl.ds(pl.multiple_of(index * LANES, LANES), LANES)
    left_ref[:N, columns] = high
    left_ref[N:, columns] = low


def act_on(left_ref, high_ref, low_ref):
    both = dot(left_ref[...], high_ref[...])
    return both[:N] + both[N:] + dot(left_ref[:N], low_ref[...])


def arrange_kernel(core_ref, raw_ref, out_ref, plain_ref, mine_ref):
    left = is_left(N // 2)
    is_first = core_ref[0] == 0
    for pair in range(PAIRS):
        one = raw_ref[pl.ds(2 * pair, N // 2, stride=G), :]
        two = raw_ref[pl.ds(2 * pair + 1, N // 2, stride=G), :]
        even = jnp.where(left, one, pltpu.roll(two, N, 1))
        odd = jnp.where(left, pltpu.roll(one, N, 1), two)
        plain_ref[pl.ds(pair * N, N // 2, stride=2), :] = even
        plain_ref[pl.ds(pair * N + 1, N // 2, stride=2), :] = odd
        mine_ref[pair * N : pair * N + N // 2, :] = jnp.where(is_first, even, odd)
        mine_ref[pair * N + N // 2 : (pair + 1) * N, :] = jnp.where(is_first, odd, even)
    for q in range(STATES):
        out_ref[q] = plain_ref[...]


def own_kernel(v_ref, a_ref, ap_ref, h3_ref, h2_ref,
               act_ref, mine_ref, other_ref, ops_ref, left_ref, wh_ref, wl_ref):
    spread(h3_ref, ops_ref)
    left = split_lanes(a_ref[...])

    def own_terms(j, carry):
        for u in range(UNROLL):
            t = j * UNROLL + u
            product = dot_nt(left, tile_nt(ops_ref[t]))
            put_term(product, [v_ref[t, g] for g in range(G)], t, wh_ref, wl_ref)
        return carry

    lax.fori_loop(0, CHUNKS, own_terms, 0)
    wide = jnp.concatenate([ap_ref[p * N : (p + 1) * N, :] for p in range(PAIRS)], axis=1)
    high, low = split(wide)
    rows_both = jnp.concatenate([high, low], axis=0)
    for j in range(CHUNKS):
        part = slice(j * UNROLL * N, (j + 1) * UNROLL * N)
        both = dot_nt(rows_both, wh_ref[part, :])
        field = both[:N] + both[N:] + dot_nt(high, wl_ref[part, :])
        for half in range(2):
            lanes = slice(half * LANES, (half + 1) * LANES)
            rows = slice((2 * j + half) * N // 2, (2 * j + half + 1) * N // 2)
            mine_ref[rows, :] = field[: N // 2, lanes]
            other_ref[rows, :] = field[N // 2 :, lanes]

    spread(h2_ref, ops_ref)
    for i in range(OWN_TILES):
        put_left((ops_ref[2 * i], ops_ref[2 * i + 1]), i, left_ref)
    act_ref[...] = act_on(left_ref, wh_ref, wl_ref)


def turned_kernel(cv_ref, ap_ref, c3_ref, zh_hbm, zl_hbm, ops_ref, zh_ref, zl_ref, sems):
    def chunk_copies(j):
        rows = pl.ds(pl.multiple_of(j * UNROLL * N, UNROLL * N), UNROLL * N)
        return [
            pltpu.make_async_copy(zh_ref.at[rows, :], zh_hbm.at[rows, :], sems.at[0, j]),
            pltpu.make_async_copy(zl_ref.at[rows, :], zl_hbm.at[rows, :], sems.at[1, j]),
        ]

    left_p = split_lanes(ap_ref[...])
    spread(c3_ref, ops_ref)

    def coupling_terms(j, carry):
        for u in range(UNROLL):
            k = j * UNROLL + u
            product = dot(left_p, tile_nn(ops_ref[k]))
            put_term(product, [cv_ref[k, g] for g in range(G)], k, zh_ref, zl_ref)

        @pl.when(j > 0)
        def _():
            for copy in chunk_copies(j - 1):
                copy.start()

        return carry

    lax.fori_loop(0, CHUNKS, coupling_terms, 0)
    for j in range(CHUNKS - 1):
        for copy in chunk_copies(j):
            copy.wait()
    for copy in chunk_copies(CHUNKS - 1):
        copy.start()
    for copy in chunk_copies(CHUNKS - 1):
        copy.wait()


def field_kernel(source_ref, term_ref, valid_ref, all_ref, zh_hbm, zl_hbm,
                 mine_ref, other_ref, gh_ref, gl_ref, zh_ref, zl_ref, f_ref, sems):
    def chunk_copies(j):
        rows = pl.ds(pl.multiple_of(j * UNROLL * N, UNROLL * N), UNROLL * N)
        return [
            pltpu.make_async_copy(zh_hbm.at[rows, :], zh_ref.at[rows, :], sems.at[0, j]),
            pltpu.make_async_copy(zl_hbm.at[rows, :], zl_ref.at[rows, :], sems.at[1, j]),
        ]

    for j in range(CHUNKS):
        for copy in chunk_copies(j):
            copy.start()
    for q in range(STATES):
        for pair in range(PAIRS):
            high, low = split(all_ref[q, pair * N : (pair + 1) * N, :])
            lanes = slice(pair * LANES, (pair + 1) * LANES)
            gh_ref[q * N : (q + 1) * N, lanes] = high
            gl_ref[q * N : (q + 1) * N, lanes] = low
    def block(j, carry):
        for copy in chunk_copies(2 * j) + chunk_copies(2 * j + 1):
            copy.wait()
        rows = pl.ds(pl.multiple_of(j * 2 * UNROLL * N, 2 * UNROLL * N), 2 * UNROLL * N)
        zh = zh_ref[rows, :]
        left = jnp.concatenate([zh, zl_ref[rows, :], zh], axis=1)
        for half in range(2):
            here = slice(half * 4 * N, (half + 1) * 4 * N)
            gh = gh_ref[here, :]
            right = jnp.concatenate([gh, gh, gl_ref[here, :]], axis=1)
            product = dot_nt(left, right)
            f_ref[2 * half, rows, :] = product[:, :LANES]
            f_ref[2 * half + 1, rows, :] = product[:, LANES:]
        return carry

    lax.fori_loop(0, CHUNKS // 2, block, 0)
    left_lanes = is_left(N)

    def pick(slot):
        source = source_ref[slot]
        rows = pl.ds(pl.multiple_of(term_ref[slot] * N, N), N)
        return f_ref[source // 2, rows, :], lax.rem(source, 2)

    def slot_pair(i):
        first, odd_first = pick(2 * i)
        second, odd_second = pick(2 * i + 1)
        first = jnp.where(odd_first == 1, pltpu.roll(first, N, 1), first)
        second = jnp.where(odd_second == 0, pltpu.roll(second, N, 1), second)
        first = jnp.where(valid_ref[2 * i] == 1, first, 0.0)
        second = jnp.where(valid_ref[2 * i + 1] == 1, second, 0.0)
        field = jnp.where(left_lanes, first, second)
        where_to = pl.ds(i, N // 2, stride=PAIR_TILES)
        mine_ref[where_to, :] = field[: N // 2]
        other_ref[where_to, :] = field[N // 2 :]

    def slot_pairs(i, carry):
        for u in range(PAIR_TILES // 2):
            slot_pair(PAIR_TILES // 2 * i + u)
        return carry

    lax.fori_loop(0, 2, slot_pairs, 0)


def pair_kernel(source_ref, term_ref, valid_ref, cv_ref, all_ref, c3_ref, c2_ref, act_ref,
                out_ref, left_all_ref, ops_ref, left_ref, wh_ref, wl_ref, sum_ref):
    for q in range(STATES):
        left_all_ref[q] = split_lanes(all_ref[q])
    spread(c2_ref, ops_ref)

    def left_tiles(i, carry):
        for u in range(2):
            tile = 2 * i + u
            first, second = term_ref[2 * tile], term_ref[2 * tile + 1]
            put_left((ops_ref[first], ops_ref[second]), tile, left_ref)
        return carry

    lax.fori_loop(0, SLOTS // 4, left_tiles, 0)
    spread(c3_ref, ops_ref)

    def slot_terms(j, carry):
        for u in range(UNROLL):
            slot = j * UNROLL + u
            k = term_ref[slot]
            product = dot_nt(left_all_ref[source_ref[slot]], tile_nt(ops_ref[k]))
            is_valid = valid_ref[slot] == 1
            weights = [jnp.where(is_valid, cv_ref[k, g], 0.0) for g in range(G)]
            put_term(product, weights, slot, wh_ref, wl_ref)
        return carry

    lax.fori_loop(0, SLOTS // UNROLL, slot_terms, 0)
    action = act_ref[...] + act_on(left_ref, wh_ref, wl_ref)
    left = is_left(N // 2)
    for pair in range(PAIRS):
        sum_ref[pair * N : (pair + 1) * N, :] = action[:, pair * LANES : (pair + 1) * LANES]
        even = sum_ref[pl.ds(pair * N, N // 2, stride=2), :]
        odd = sum_ref[pl.ds(pair * N + 1, N // 2, stride=2), :]
        one = jnp.where(left, even, pltpu.roll(odd, N, 1))
        two = jnp.where(left, pltpu.roll(even, N, 1), odd)
        out_ref[pl.ds(2 * pair, N // 2, stride=G), :] = one
        out_ref[pl.ds(2 * pair + 1, N // 2, stride=G), :] = two


def merge_kernel(mine_ref, theirs_ref, own_ref, out_ref):
    for a in range(N // 2):
        here = slice(a * PAIR_TILES, (a + 1) * PAIR_TILES)
        out_ref[a * ALL_TILES : a * ALL_TILES + PAIR_TILES, :] = mine_ref[here, :] + theirs_ref[here, :]
    for r in range(LAST_TILES):
        out_ref[pl.ds(PAIR_TILES + r, N // 2, stride=ALL_TILES), :] = own_ref[r]


def total_kernel(parts_ref, own_ref, pair_ref):
    def part(i, first, count):
        return parts_ref[i * ALL_TILES + first : i * ALL_TILES + first + count, :]

    total = part(0, 0, PAIR_TILES)
    for i in range(1, N // 2):
        total = total + part(i, 0, PAIR_TILES)
    pair_ref[...] = total
    for x in range(X_CHIPS):
        total = part(x, PAIR_TILES, LAST_TILES)
        for z in range(1, N // 2 // X_CHIPS):
            total = total + part(z * X_CHIPS + x, PAIR_TILES, LAST_TILES)
        own_ref[x * LAST_TILES : (x + 1) * LAST_TILES, :] = total


def shape(*dims, dtype=F32):
    return jax.ShapeDtypeStruct(dims, dtype)


def cost(flops, nbytes):
    return pl.CostEstimate(flops=flops, bytes_accessed=nbytes, transcendentals=0)


def params(mib):
    return pltpu.CompilerParams(vmem_limit_bytes=mib << 20)


OWN_GRANT = 52
FIELD_GRANT = 52


def arrange(core, raw):
    return pl.pallas_call(
        arrange_kernel,
        out_shape=(shape(STATES, PAIRS * N, LANES), shape(PAIRS * N, LANES), shape(PAIRS * N, LANES)),
        in_specs=[SMEM, VMEM],
        out_specs=[pl.BlockSpec(), VMEM, VMEM],
        compiler_params=params(8),
        name="arrange",
    )(core, raw)


def own_part(v, a2, a2p, h3, h2):
    big = pltpu.VMEM((TERMS * N, G * N), BF16)
    return pl.pallas_call(
        own_kernel,
        out_shape=(
            shape(N, G * N),
            shape(N // 2 * OWN_TILES, LANES),
            shape(N // 2 * OWN_TILES, LANES),
        ),
        in_specs=[SMEM] + [VMEM] * 4,
        out_specs=[VMEM] * 3,
        scratch_shapes=[
            pltpu.VMEM((TERMS, N, LANES), F32),
            pltpu.VMEM((LANES, TERMS * N), BF16),
            big, big,
        ],
        compiler_params=params(24),
        cost_estimate=cost(2_000_000_000, 4 << 20),
        name="own_part",
    )(v, a2, a2p, h3, h2)


def turned(cv, a2p, c3):
    big = pltpu.VMEM((TERMS * N, G * N), BF16)
    return pl.pallas_call(
        turned_kernel,
        out_shape=(
            shape(TERMS * N, G * N, dtype=BF16),
            shape(TERMS * N, G * N, dtype=BF16),
        ),
        in_specs=[SMEM] + [VMEM] * 2,
        out_specs=[HBM] * 2,
        scratch_shapes=[
            pltpu.VMEM((TERMS, N, LANES), F32),
            big, big,
            pltpu.SemaphoreType.DMA((2, CHUNKS)),
        ],
        compiler_params=params(OWN_GRANT),
        cost_estimate=cost(1_000_000_000, 6 << 20),
        name="turned",
    )(cv, a2p, c3)


def pair_fields(source, term, valid, everyone, zh, zl):
    big = pltpu.VMEM((TERMS * N, G * N), BF16)
    rows = N // 2 * PAIR_TILES
    return pl.pallas_call(
        field_kernel,
        out_shape=(shape(rows, LANES), shape(rows, LANES)),
        in_specs=[SMEM] * 3 + [VMEM] + [HBM] * 2,
        out_specs=[VMEM] * 2,
        scratch_shapes=[
            pltpu.VMEM((STATES * N, G * N), BF16),
            pltpu.VMEM((STATES * N, G * N), BF16),
            big, big,
            pltpu.VMEM((STATES // 2, TERMS * N, LANES), F32),
            pltpu.SemaphoreType.DMA((2, CHUNKS)),
        ],
        compiler_params=params(FIELD_GRANT),
        cost_estimate=cost(3_000_000_000, 6 << 20),
        name="pair_fields",
    )(source, term, valid, everyone, zh, zl)


def pair_action(source, term, valid, cv, everyone, c3, c2, act):
    return pl.pallas_call(
        pair_kernel,
        out_shape=shape(PAIRS * N, LANES),
        in_specs=[SMEM] * 4 + [VMEM] * 4,
        out_specs=pl.BlockSpec(),
        scratch_shapes=[
            pltpu.VMEM((STATES, PAIRS * N, 2 * LANES), BF16),
            pltpu.VMEM((TERMS, N, LANES), F32),
            pltpu.VMEM((LANES, SLOTS * N), BF16),
            pltpu.VMEM((SLOTS * N, G * N), BF16),
            pltpu.VMEM((SLOTS * N, G * N), BF16),
            pltpu.VMEM((PAIRS * N, LANES), F32),
        ],
        compiler_params=params(24),
        cost_estimate=cost(3_000_000_000, 4 << 20),
        name="pair_action",
    )(source, term, valid, cv, everyone, c3, c2, act)


def merge(mine, theirs, own):
    return pl.pallas_call(
        merge_kernel,
        out_shape=shape(N // 2 * ALL_TILES, LANES),
        in_specs=[VMEM] * 3,
        out_specs=pl.BlockSpec(),
        compiler_params=params(8),
        name="merge",
    )(mine, theirs, own)


def total(parts):
    return pl.pallas_call(
        total_kernel,
        out_shape=(shape(OWN_TILES, LANES), shape(PAIR_TILES, LANES)),
        in_specs=[pl.BlockSpec()],
        out_specs=(pl.BlockSpec(), pl.BlockSpec()),
        compiler_params=params(8),
        name="total",
    )(parts)


def tile_rows(flat):
    blocks = flat.shape[0] // 8
    tiles = flat.reshape(blocks, 8, N // 2, LANES)
    return tiles.transpose(0, 2, 1, 3).reshape(blocks * 8 * N // 2, LANES)


def read_list(pairs, myself):
    is_mine = pairs[:, 0] == myself
    rank = jnp.cumsum(is_mine.astype(jnp.int32)) - 1
    slots = jnp.arange(SLOTS, dtype=jnp.int32)
    picked = (rank[None, :] == slots[:, None]) & is_mine[None, :]
    source = jnp.sum(jnp.where(picked, pairs[None, :, 1], 0), axis=1)
    term = jnp.sum(jnp.where(picked, pairs[None, :, 2], 0), axis=1)
    valid = jnp.sum(picked.astype(jnp.int32), axis=1)
    return source, term, valid


def other_core(value):
    return lax.ppermute(value, "core", [(0, 1), (1, 0)])


def reduce_own(mine, other):
    x = lax.axis_index("x")
    tiles = (mine + other_core(other)).reshape(2, 2, LAST_TILES, N // 2, LANES)
    for axis, bit in ((1, 1), (0, 2)):
        mine_here = (x // bit) % 2
        keep = lax.dynamic_index_in_dim(tiles, mine_here, axis, False)
        send = lax.dynamic_index_in_dim(tiles, 1 - mine_here, axis, False)
        tiles = keep + lax.ppermute(send, "x", [(i, i ^ bit) for i in range(X_CHIPS)])
    return tiles


def per_device(coeffs, diag_h2, diag_h3, diag_v1, coup_h2, coup_h3, coup_v1, pairs):
    core = lax.axis_index("core").astype(jnp.int32)[None]
    to_all, plain, mine_first = arrange(core, tile_rows(coeffs[0]))
    everyone = lax.all_to_all(to_all, "state", 0, 0, tiled=True)
    listed = read_list(pairs, lax.axis_index("state"))
    c3 = tile_rows(coup_h3)
    act, own_mine, own_other = own_part(
        diag_v1[0], plain, mine_first, tile_rows(diag_h3[0]), tile_rows(diag_h2[0])
    )
    zh, zl = turned(coup_v1, mine_first, c3)
    everyone, own_columns = lax.optimization_barrier(
        (everyone, reduce_own(own_mine, own_other))
    )
    pair_mine, pair_other = pair_fields(*listed, everyone, zh, zl)
    sums = merge(pair_mine, other_core(pair_other), own_columns)
    parts = lax.all_to_all(
        sums.reshape(N // 2, 1, ALL_TILES * LANES), ("z", "x"), 0, 0, tiled=True
    )
    out = pair_action(*listed, coup_v1, everyone, c3, tile_rows(coup_h2), act)
    action = out.reshape(N // 2, G, LANES).transpose(1, 0, 2).reshape(1, G, N * N)
    own_row, pair_row = total(parts.reshape(N // 2 * ALL_TILES, LANES))
    return action, own_row.reshape(1, 1, TERMS * N), pair_row.reshape(1, 1, SLOTS * N)


def solution(mesh):
    fine = Mesh(mesh.devices.reshape(8, 8, 4, 2), ("state", "z", "x", "core"))
    mode = ("z", "x", "core")
    placed = (
        P("state", mode, None),
        P("state", None, None),
        P("state", None, None),
        P("state", None, mode),
        P(),
        P(),
        P(None, mode),
        P(),
    )
    out = P("state", mode, None)
    return jax.shard_map(
        per_device, mesh=fine, in_specs=placed, out_specs=(out, out, out), check_vma=False
    )
```

```python
import jax
import jax.numpy as jnp
from jax import lax
from jax.experimental import pallas as pl
from jax.experimental.pallas import tpu as pltpu
from jax.sharding import Mesh, PartitionSpec as P

N = 64
G = 8
PAIRS = G // 2
LANES = 2 * N
TERMS = 32
STATES = 8
SLOTS = 48
OWN_TILES = TERMS // 2
PAIR_TILES = SLOTS // 2
X_CHIPS = 4
LAST_TILES = OWN_TILES // X_CHIPS
ALL_TILES = PAIR_TILES + LAST_TILES
UNROLL = 4
CHUNKS = TERMS // 4
HELD_TERMS = 8
SENT_TERMS = TERMS - HELD_TERMS
SENT_CHUNKS = SENT_TERMS // UNROLL
F32 = jnp.float32
BF16 = jnp.bfloat16
NT = (((1,), (1,)), ((), ()))
VMEM = pl.BlockSpec(memory_space=pltpu.VMEM)
SMEM = pl.BlockSpec(memory_space=pltpu.SMEM)
HBM = pl.BlockSpec(memory_space=pltpu.HBM)


def dot(left, right):
    return jnp.dot(left, right, preferred_element_type=F32)


def dot_nt(left, right):
    return lax.dot_general(left, right, NT, preferred_element_type=F32)


def is_left(rows):
    return lax.broadcasted_iota(jnp.int32, (rows, LANES), 1) < N


def split(value):
    high = value.astype(BF16)
    low = (value - high.astype(F32)).astype(BF16)
    return high, low


def split_lanes(value):
    return jnp.concatenate(split(value), axis=1)


def half_blocks(operator):
    left = is_left(N)
    high = operator.astype(BF16).astype(F32)
    low = operator - high
    zero = jnp.zeros_like(operator)
    return [
        jnp.where(left, high, zero).astype(BF16),
        jnp.where(left, zero, high).astype(BF16),
        jnp.where(left, low, zero).astype(BF16),
        jnp.where(left, zero, low).astype(BF16),
    ]


def tile_nt(operator):
    h0, h1, l0, l1 = half_blocks(operator)
    zero = jnp.zeros((LANES, LANES), BF16)
    high = jnp.concatenate([h0, h1], axis=0)
    low = jnp.concatenate([l0, l1], axis=0)
    return jnp.concatenate(
        [jnp.concatenate([high, low], axis=0), jnp.concatenate([high, zero], axis=0)], axis=1
    )


def tile_nn(operator):
    h0, h1, l0, l1 = half_blocks(operator)
    zero = jnp.zeros((LANES, LANES), BF16)
    high = jnp.concatenate([h0, h1], axis=0)
    low = jnp.concatenate([l0, l1], axis=0)
    return jnp.concatenate(
        [jnp.concatenate([high, low], axis=1), jnp.concatenate([high, zero], axis=1)], axis=0
    )


def spread(raw_ref, out_ref):
    left = is_left(N // 2)
    for t in range(TERMS):
        start = (t // 8) * (8 * N // 2) + t % 8
        value = raw_ref[pl.ds(start, N // 2, stride=8), :]
        turned = pltpu.roll(value, N, 1)
        out_ref[t, pl.ds(0, N // 2, stride=2), :] = jnp.where(left, value, turned)
        out_ref[t, pl.ds(1, N // 2, stride=2), :] = jnp.where(left, turned, value)


def put_term(product, weights, index, high_ref, low_ref):
    value = product[:, :LANES] + product[:, LANES:]
    rows = pl.ds(pl.multiple_of(index * N, N), N)
    left = is_left(1)
    for pair in range(PAIRS):
        weight = jnp.where(left, weights[2 * pair], weights[2 * pair + 1])
        high, low = split(value[pair * N : (pair + 1) * N] * weight)
        high_ref[rows, pair * LANES : (pair + 1) * LANES] = high
        low_ref[rows, pair * LANES : (pair + 1) * LANES] = low


def put_left(operators, index, left_ref):
    high, low = split(jnp.where(is_left(N), operators[0], operators[1]))
    columns = pl.ds(pl.multiple_of(index * LANES, LANES), LANES)
    left_ref[:N, columns] = high
    left_ref[N:, columns] = low


def act_on(left_ref, high_ref, low_ref):
    both = dot(left_ref[...], high_ref[...])
    return both[:N] + both[N:] + dot(left_ref[:N], low_ref[...])


def arrange_kernel(core_ref, raw_ref, out_ref, plain_ref, mine_ref):
    left = is_left(N // 2)
    is_first = core_ref[0] == 0
    for pair in range(PAIRS):
        one = raw_ref[pl.ds(2 * pair, N // 2, stride=G), :]
        two = raw_ref[pl.ds(2 * pair + 1, N // 2, stride=G), :]
        even = jnp.where(left, one, pltpu.roll(two, N, 1))
        odd = jnp.where(left, pltpu.roll(one, N, 1), two)
        plain_ref[pl.ds(pair * N, N // 2, stride=2), :] = even
        plain_ref[pl.ds(pair * N + 1, N // 2, stride=2), :] = odd
        mine_ref[pair * N : pair * N + N // 2, :] = jnp.where(is_first, even, odd)
        mine_ref[pair * N + N // 2 : (pair + 1) * N, :] = jnp.where(is_first, odd, even)
    for q in range(STATES):
        out_ref[q] = plain_ref[...]


def own_kernel(v_ref, a_ref, ap_ref, h3_ref, h2_ref,
               act_ref, mine_ref, other_ref, ops_ref, left_ref, wh_ref, wl_ref):
    spread(h3_ref, ops_ref)
    left = split_lanes(a_ref[...])

    def own_terms(j, carry):
        for u in range(UNROLL):
            t = j * UNROLL + u
            product = dot_nt(left, tile_nt(ops_ref[t]))
            put_term(product, [v_ref[t, g] for g in range(G)], t, wh_ref, wl_ref)
        return carry

    lax.fori_loop(0, CHUNKS, own_terms, 0)
    wide = jnp.concatenate([ap_ref[p * N : (p + 1) * N, :] for p in range(PAIRS)], axis=1)
    high, low = split(wide)
    rows_both = jnp.concatenate([high, low], axis=0)
    for j in range(CHUNKS):
        part = slice(j * UNROLL * N, (j + 1) * UNROLL * N)
        both = dot_nt(rows_both, wh_ref[part, :])
        field = both[:N] + both[N:] + dot_nt(high, wl_ref[part, :])
        for half in range(2):
            lanes = slice(half * LANES, (half + 1) * LANES)
            rows = slice((2 * j + half) * N // 2, (2 * j + half + 1) * N // 2)
            mine_ref[rows, :] = field[: N // 2, lanes]
            other_ref[rows, :] = field[N // 2 :, lanes]

    spread(h2_ref, ops_ref)
    for i in range(OWN_TILES):
        put_left((ops_ref[2 * i], ops_ref[2 * i + 1]), i, left_ref)
    act_ref[...] = act_on(left_ref, wh_ref, wl_ref)


def turned_kernel(cv_ref, ap_ref, c3_ref, zh0_ref, zl0_ref, zh_hbm, zl_hbm,
                  ops_ref, zh_ref, zl_ref, sems):
    def chunk_copies(j):
        rows = pl.ds(pl.multiple_of(j * UNROLL * N, UNROLL * N), UNROLL * N)
        return [
            pltpu.make_async_copy(zh_ref.at[rows, :], zh_hbm.at[rows, :], sems.at[0, j]),
            pltpu.make_async_copy(zl_ref.at[rows, :], zl_hbm.at[rows, :], sems.at[1, j]),
        ]

    left_p = split_lanes(ap_ref[...])
    spread(c3_ref, ops_ref)

    def coupling_term(k, high_ref, low_ref, index):
        product = dot(left_p, tile_nn(ops_ref[k]))
        put_term(product, [cv_ref[k, g] for g in range(G)], index, high_ref, low_ref)

    def sent_terms(j, carry):
        for u in range(UNROLL):
            coupling_term(HELD_TERMS + j * UNROLL + u, zh_ref, zl_ref, j * UNROLL + u)

        @pl.when(j > 0)
        def _():
            for copy in chunk_copies(j - 1):
                copy.start()

        return carry

    def held_terms(j, carry):
        for u in range(UNROLL):
            coupling_term(j * UNROLL + u, zh0_ref, zl0_ref, j * UNROLL + u)
        return carry

    lax.fori_loop(0, SENT_CHUNKS, sent_terms, 0)
    lax.fori_loop(0, 1, held_terms, 0)
    for copy in chunk_copies(SENT_CHUNKS - 1):
        copy.start()
    lax.fori_loop(1, HELD_TERMS // UNROLL, held_terms, 0)
    for j in range(SENT_CHUNKS):
        for copy in chunk_copies(j):
            copy.wait()


def field_kernel(source_ref, term_ref, valid_ref, all_ref, zh0_ref, zl0_ref, zh_hbm, zl_hbm,
                 mine_ref, other_ref, gh_ref, gl_ref, zh_ref, zl_ref, f_ref, sems):
    def chunk_copies(j):
        rows = pl.ds(pl.multiple_of(j * UNROLL * N, UNROLL * N), UNROLL * N)
        return [
            pltpu.make_async_copy(zh_hbm.at[rows, :], zh_ref.at[rows, :], sems.at[0, j]),
            pltpu.make_async_copy(zl_hbm.at[rows, :], zl_ref.at[rows, :], sems.at[1, j]),
        ]

    for j in range(SENT_CHUNKS):
        for copy in chunk_copies(j):
            copy.start()
    for q in range(STATES):
        for pair in range(PAIRS):
            high, low = split(all_ref[q, pair * N : (pair + 1) * N, :])
            lanes = slice(pair * LANES, (pair + 1) * LANES)
            gh_ref[q * N : (q + 1) * N, lanes] = high
            gl_ref[q * N : (q + 1) * N, lanes] = low
    def block(zh, zl, rows):
        left = jnp.concatenate([zh, zl, zh], axis=1)
        for half in range(2):
            here = slice(half * 4 * N, (half + 1) * 4 * N)
            gh = gh_ref[here, :]
            right = jnp.concatenate([gh, gh, gl_ref[here, :]], axis=1)
            product = dot_nt(left, right)
            f_ref[2 * half, rows, :] = product[:, :LANES]
            f_ref[2 * half + 1, rows, :] = product[:, LANES:]

    def sent_block(j, carry):
        for copy in chunk_copies(2 * j) + chunk_copies(2 * j + 1):
            copy.wait()
        size = 2 * UNROLL * N
        rows = pl.ds(pl.multiple_of(j * size, size), size)
        to_rows = pl.ds(pl.multiple_of((j + 1) * size, size), size)
        block(zh_ref[rows, :], zl_ref[rows, :], to_rows)
        return carry

    block(zh0_ref[...], zl0_ref[...], slice(0, HELD_TERMS * N))
    lax.fori_loop(0, SENT_CHUNKS // 2, sent_block, 0)
    left_lanes = is_left(N)

    def pick(slot):
        source = source_ref[slot]
        rows = pl.ds(pl.multiple_of(term_ref[slot] * N, N), N)
        return f_ref[source // 2, rows, :], lax.rem(source, 2)

    def slot_pair(i):
        first, odd_first = pick(2 * i)
        second, odd_second = pick(2 * i + 1)
        first = jnp.where(odd_first == 1, pltpu.roll(first, N, 1), first)
        second = jnp.where(odd_second == 0, pltpu.roll(second, N, 1), second)
        first = jnp.where(valid_ref[2 * i] == 1, first, 0.0)
        second = jnp.where(valid_ref[2 * i + 1] == 1, second, 0.0)
        field = jnp.where(left_lanes, first, second)
        where_to = pl.ds(i, N // 2, stride=PAIR_TILES)
        mine_ref[where_to, :] = field[: N // 2]
        other_ref[where_to, :] = field[N // 2 :]

    def slot_pairs(i, carry):
        for u in range(PAIR_TILES // 2):
            slot_pair(PAIR_TILES // 2 * i + u)
        return carry

    lax.fori_loop(0, 2, slot_pairs, 0)


def pair_kernel(source_ref, term_ref, valid_ref, cv_ref, all_ref, c3_ref, c2_ref, act_ref,
                out_ref, left_all_ref, ops_ref, left_ref, wh_ref, wl_ref, sum_ref):
    for q in range(STATES):
        left_all_ref[q] = split_lanes(all_ref[q])
    spread(c2_ref, ops_ref)

    def left_tiles(i, carry):
        for u in range(2):
            tile = 2 * i + u
            first, second = term_ref[2 * tile], term_ref[2 * tile + 1]
            put_left((ops_ref[first], ops_ref[second]), tile, left_ref)
        return carry

    lax.fori_loop(0, SLOTS // 4, left_tiles, 0)
    spread(c3_ref, ops_ref)

    def slot_terms(j, carry):
        for u in range(UNROLL):
            slot = j * UNROLL + u
            k = term_ref[slot]
            product = dot_nt(left_all_ref[source_ref[slot]], tile_nt(ops_ref[k]))
            is_valid = valid_ref[slot] == 1
            weights = [jnp.where(is_valid, cv_ref[k, g], 0.0) for g in range(G)]
            put_term(product, weights, slot, wh_ref, wl_ref)
        return carry

    lax.fori_loop(0, SLOTS // UNROLL, slot_terms, 0)
    action = act_ref[...] + act_on(left_ref, wh_ref, wl_ref)
    left = is_left(N // 2)
    for pair in range(PAIRS):
        sum_ref[pair * N : (pair + 1) * N, :] = action[:, pair * LANES : (pair + 1) * LANES]
        even = sum_ref[pl.ds(pair * N, N // 2, stride=2), :]
        odd = sum_ref[pl.ds(pair * N + 1, N // 2, stride=2), :]
        one = jnp.where(left, even, pltpu.roll(odd, N, 1))
        two = jnp.where(left, pltpu.roll(even, N, 1), odd)
        out_ref[pl.ds(2 * pair, N // 2, stride=G), :] = one
        out_ref[pl.ds(2 * pair + 1, N // 2, stride=G), :] = two


def merge_kernel(mine_ref, theirs_ref, own_ref, out_ref):
    for a in range(N // 2):
        here = slice(a * PAIR_TILES, (a + 1) * PAIR_TILES)
        out_ref[a * ALL_TILES : a * ALL_TILES + PAIR_TILES, :] = mine_ref[here, :] + theirs_ref[here, :]
    for r in range(LAST_TILES):
        out_ref[pl.ds(PAIR_TILES + r, N // 2, stride=ALL_TILES), :] = own_ref[r]


def total_kernel(parts_ref, own_ref, pair_ref):
    def part(i, first, count):
        return parts_ref[i * ALL_TILES + first : i * ALL_TILES + first + count, :]

    total = part(0, 0, PAIR_TILES)
    for i in range(1, N // 2):
        total = total + part(i, 0, PAIR_TILES)
    pair_ref[...] = total
    for x in range(X_CHIPS):
        total = part(x, PAIR_TILES, LAST_TILES)
        for z in range(1, N // 2 // X_CHIPS):
            total = total + part(z * X_CHIPS + x, PAIR_TILES, LAST_TILES)
        own_ref[x * LAST_TILES : (x + 1) * LAST_TILES, :] = total


def shape(*dims, dtype=F32):
    return jax.ShapeDtypeStruct(dims, dtype)


def cost(flops, nbytes):
    return pl.CostEstimate(flops=flops, bytes_accessed=nbytes, transcendentals=0)


def params(mib):
    return pltpu.CompilerParams(vmem_limit_bytes=mib << 20)


OWN_GRANT = 52
FIELD_GRANT = 51


def arrange(core, raw):
    return pl.pallas_call(
        arrange_kernel,
        out_shape=(shape(STATES, PAIRS * N, LANES), shape(PAIRS * N, LANES), shape(PAIRS * N, LANES)),
        in_specs=[SMEM, VMEM],
        out_specs=[pl.BlockSpec(), VMEM, VMEM],
        compiler_params=params(8),
        name="arrange",
    )(core, raw)


def own_part(v, a2, a2p, h3, h2):
    big = pltpu.VMEM((TERMS * N, G * N), BF16)
    return pl.pallas_call(
        own_kernel,
        out_shape=(
            shape(N, G * N),
            shape(N // 2 * OWN_TILES, LANES),
            shape(N // 2 * OWN_TILES, LANES),
        ),
        in_specs=[SMEM] + [VMEM] * 4,
        out_specs=[VMEM] * 3,
        scratch_shapes=[
            pltpu.VMEM((TERMS, N, LANES), F32),
            pltpu.VMEM((LANES, TERMS * N), BF16),
            big, big,
        ],
        compiler_params=params(24),
        cost_estimate=cost(2_000_000_000, 4 << 20),
        name="own_part",
    )(v, a2, a2p, h3, h2)


def turned(cv, a2p, c3):
    big = pltpu.VMEM((SENT_TERMS * N, G * N), BF16)
    return pl.pallas_call(
        turned_kernel,
        out_shape=(
            shape(HELD_TERMS * N, G * N, dtype=BF16),
            shape(HELD_TERMS * N, G * N, dtype=BF16),
            shape(SENT_TERMS * N, G * N, dtype=BF16),
            shape(SENT_TERMS * N, G * N, dtype=BF16),
        ),
        in_specs=[SMEM] + [VMEM] * 2,
        out_specs=[VMEM] * 2 + [HBM] * 2,
        scratch_shapes=[
            pltpu.VMEM((TERMS, N, LANES), F32),
            big, big,
            pltpu.SemaphoreType.DMA((2, SENT_CHUNKS)),
        ],
        compiler_params=params(OWN_GRANT),
        cost_estimate=cost(1_000_000_000, 6 << 20),
        name="turned",
    )(cv, a2p, c3)


def pair_fields(source, term, valid, everyone, z):
    big = pltpu.VMEM((SENT_TERMS * N, G * N), BF16)
    rows = N // 2 * PAIR_TILES
    return pl.pallas_call(
        field_kernel,
        out_shape=(shape(rows, LANES), shape(rows, LANES)),
        in_specs=[SMEM] * 3 + [VMEM] * 3 + [HBM] * 2,
        out_specs=[VMEM] * 2,
        scratch_shapes=[
            pltpu.VMEM((STATES * N, G * N), BF16),
            pltpu.VMEM((STATES * N, G * N), BF16),
            big, big,
            pltpu.VMEM((STATES // 2, TERMS * N, LANES), F32),
            pltpu.SemaphoreType.DMA((2, SENT_CHUNKS)),
        ],
        compiler_params=params(FIELD_GRANT),
        cost_estimate=cost(3_000_000_000, 6 << 20),
        name="pair_fields",
    )(source, term, valid, everyone, *z)


def pair_action(source, term, valid, cv, everyone, c3, c2, act):
    return pl.pallas_call(
        pair_kernel,
        out_shape=shape(PAIRS * N, LANES),
        in_specs=[SMEM] * 4 + [VMEM] * 4,
        out_specs=pl.BlockSpec(),
        scratch_shapes=[
            pltpu.VMEM((STATES, PAIRS * N, 2 * LANES), BF16),
            pltpu.VMEM((TERMS, N, LANES), F32),
            pltpu.VMEM((LANES, SLOTS * N), BF16),
            pltpu.VMEM((SLOTS * N, G * N), BF16),
            pltpu.VMEM((SLOTS * N, G * N), BF16),
            pltpu.VMEM((PAIRS * N, LANES), F32),
        ],
        compiler_params=params(24),
        cost_estimate=cost(3_000_000_000, 4 << 20),
        name="pair_action",
    )(source, term, valid, cv, everyone, c3, c2, act)


def merge(mine, theirs, own):
    return pl.pallas_call(
        merge_kernel,
        out_shape=shape(N // 2 * ALL_TILES, LANES),
        in_specs=[VMEM] * 3,
        out_specs=pl.BlockSpec(),
        compiler_params=params(8),
        name="merge",
    )(mine, theirs, own)


def total(parts):
    return pl.pallas_call(
        total_kernel,
        out_shape=(shape(OWN_TILES, LANES), shape(PAIR_TILES, LANES)),
        in_specs=[pl.BlockSpec()],
        out_specs=(pl.BlockSpec(), pl.BlockSpec()),
        compiler_params=params(8),
        name="total",
    )(parts)


def tile_rows(flat):
    blocks = flat.shape[0] // 8
    tiles = flat.reshape(blocks, 8, N // 2, LANES)
    return tiles.transpose(0, 2, 1, 3).reshape(blocks * 8 * N // 2, LANES)


def read_list(pairs, myself):
    is_mine = pairs[:, 0] == myself
    rank = jnp.cumsum(is_mine.astype(jnp.int32)) - 1
    slots = jnp.arange(SLOTS, dtype=jnp.int32)
    picked = (rank[None, :] == slots[:, None]) & is_mine[None, :]
    source = jnp.sum(jnp.where(picked, pairs[None, :, 1], 0), axis=1)
    term = jnp.sum(jnp.where(picked, pairs[None, :, 2], 0), axis=1)
    valid = jnp.sum(picked.astype(jnp.int32), axis=1)
    return source, term, valid


def other_core(value):
    return lax.ppermute(value, "core", [(0, 1), (1, 0)])


def reduce_own(mine, other):
    x = lax.axis_index("x")
    tiles = (mine + other_core(other)).reshape(2, 2, LAST_TILES, N // 2, LANES)
    for axis, bit in ((1, 1), (0, 2)):
        mine_here = (x // bit) % 2
        keep = lax.dynamic_index_in_dim(tiles, mine_here, axis, False)
        send = lax.dynamic_index_in_dim(tiles, 1 - mine_here, axis, False)
        tiles = keep + lax.ppermute(send, "x", [(i, i ^ bit) for i in range(X_CHIPS)])
    return tiles


def per_device(coeffs, diag_h2, diag_h3, diag_v1, coup_h2, coup_h3, coup_v1, pairs):
    core = lax.axis_index("core").astype(jnp.int32)[None]
    to_all, plain, mine_first = arrange(core, tile_rows(coeffs[0]))
    everyone = lax.all_to_all(to_all, "state", 0, 0, tiled=True)
    listed = read_list(pairs, lax.axis_index("state"))
    c3 = tile_rows(coup_h3)
    act, own_mine, own_other = own_part(
        diag_v1[0], plain, mine_first, tile_rows(diag_h3[0]), tile_rows(diag_h2[0])
    )
    z = turned(coup_v1, mine_first, c3)
    everyone, own_columns = lax.optimization_barrier(
        (everyone, reduce_own(own_mine, own_other))
    )
    pair_mine, pair_other = pair_fields(*listed, everyone, z)
    sums = merge(pair_mine, other_core(pair_other), own_columns)
    parts = lax.all_to_all(
        sums.reshape(N // 2, 1, ALL_TILES * LANES), ("z", "x"), 0, 0, tiled=True
    )
    out = pair_action(*listed, coup_v1, everyone, c3, tile_rows(coup_h2), act)
    action = out.reshape(N // 2, G, LANES).transpose(1, 0, 2).reshape(1, G, N * N)
    own_row, pair_row = total(parts.reshape(N // 2 * ALL_TILES, LANES))
    return action, own_row.reshape(1, 1, TERMS * N), pair_row.reshape(1, 1, SLOTS * N)


def solution(mesh):
    fine = Mesh(mesh.devices.reshape(8, 8, 4, 2), ("state", "z", "x", "core"))
    mode = ("z", "x", "core")
    placed = (
        P("state", mode, None),
        P("state", None, None),
        P("state", None, None),
        P("state", None, mode),
        P(),
        P(),
        P(None, mode),
        P(),
    )
    out = P("state", mode, None)
    return jax.shard_map(
        per_device, mesh=fine, in_specs=placed, out_specs=(out, out, out), check_vma=False
    )
```

```python
import jax
import jax.numpy as jnp
from jax import lax
from jax.experimental import pallas as pl
from jax.experimental.pallas import tpu as pltpu
from jax.sharding import Mesh, PartitionSpec as P

N = 64
G = 8
PAIRS = G // 2
LANES = 2 * N
TERMS = 32
STATES = 8
SLOTS = 48
OWN_TILES = TERMS // 2
PAIR_TILES = SLOTS // 2
X_CHIPS = 4
LAST_TILES = OWN_TILES // X_CHIPS
ALL_TILES = PAIR_TILES + LAST_TILES
UNROLL = 4
CHUNKS = TERMS // 4
HELD_TERMS = 8
SENT_TERMS = TERMS - HELD_TERMS
SENT_CHUNKS = SENT_TERMS // UNROLL
F32 = jnp.float32
BF16 = jnp.bfloat16
NT = (((1,), (1,)), ((), ()))
VMEM = pl.BlockSpec(memory_space=pltpu.VMEM)
SMEM = pl.BlockSpec(memory_space=pltpu.SMEM)
HBM = pl.BlockSpec(memory_space=pltpu.HBM)


def dot(left, right):
    return jnp.dot(left, right, preferred_element_type=F32)


def dot_nt(left, right):
    return lax.dot_general(left, right, NT, preferred_element_type=F32)


def is_left(rows):
    return lax.broadcasted_iota(jnp.int32, (rows, LANES), 1) < N


def split(value):
    high = value.astype(BF16)
    low = (value - high.astype(F32)).astype(BF16)
    return high, low


def split_lanes(value):
    return jnp.concatenate(split(value), axis=1)


def half_blocks(operator):
    left = is_left(N)
    high = operator.astype(BF16).astype(F32)
    low = operator - high
    zero = jnp.zeros_like(operator)
    return [
        jnp.where(left, high, zero).astype(BF16),
        jnp.where(left, zero, high).astype(BF16),
        jnp.where(left, low, zero).astype(BF16),
        jnp.where(left, zero, low).astype(BF16),
    ]


def tile_nt(operator):
    h0, h1, l0, l1 = half_blocks(operator)
    zero = jnp.zeros((LANES, LANES), BF16)
    high = jnp.concatenate([h0, h1], axis=0)
    low = jnp.concatenate([l0, l1], axis=0)
    return jnp.concatenate(
        [jnp.concatenate([high, low], axis=0), jnp.concatenate([high, zero], axis=0)], axis=1
    )


def tile_nn(operator):
    h0, h1, l0, l1 = half_blocks(operator)
    zero = jnp.zeros((LANES, LANES), BF16)
    high = jnp.concatenate([h0, h1], axis=0)
    low = jnp.concatenate([l0, l1], axis=0)
    return jnp.concatenate(
        [jnp.concatenate([high, low], axis=1), jnp.concatenate([high, zero], axis=1)], axis=0
    )


def spread(raw_ref, out_ref):
    left = is_left(N // 2)
    for t in range(TERMS):
        start = (t // 8) * (8 * N // 2) + t % 8
        value = raw_ref[pl.ds(start, N // 2, stride=8), :]
        turned = pltpu.roll(value, N, 1)
        out_ref[t, pl.ds(0, N // 2, stride=2), :] = jnp.where(left, value, turned)
        out_ref[t, pl.ds(1, N // 2, stride=2), :] = jnp.where(left, turned, value)


def put_term(product, weights, index, high_ref, low_ref):
    value = product[:, :LANES] + product[:, LANES:]
    rows = pl.ds(pl.multiple_of(index * N, N), N)
    left = is_left(1)
    for pair in range(PAIRS):
        weight = jnp.where(left, weights[2 * pair], weights[2 * pair + 1])
        high, low = split(value[pair * N : (pair + 1) * N] * weight)
        high_ref[rows, pair * LANES : (pair + 1) * LANES] = high
        low_ref[rows, pair * LANES : (pair + 1) * LANES] = low


def put_left(operators, index, left_ref):
    high, low = split(jnp.where(is_left(N), operators[0], operators[1]))
    columns = pl.ds(pl.multiple_of(index * LANES, LANES), LANES)
    left_ref[:N, columns] = high
    left_ref[N:, columns] = low


def act_on(left_ref, high_ref, low_ref):
    both = dot(left_ref[...], high_ref[...])
    return both[:N] + both[N:] + dot(left_ref[:N], low_ref[...])


def arrange_kernel(core_ref, raw_ref, out_ref, plain_ref, mine_ref):
    left = is_left(N // 2)
    is_first = core_ref[0] == 0
    for pair in range(PAIRS):
        one = raw_ref[pl.ds(2 * pair, N // 2, stride=G), :]
        two = raw_ref[pl.ds(2 * pair + 1, N // 2, stride=G), :]
        even = jnp.where(left, one, pltpu.roll(two, N, 1))
        odd = jnp.where(left, pltpu.roll(one, N, 1), two)
        plain_ref[pl.ds(pair * N, N // 2, stride=2), :] = even
        plain_ref[pl.ds(pair * N + 1, N // 2, stride=2), :] = odd
        mine_ref[pair * N : pair * N + N // 2, :] = jnp.where(is_first, even, odd)
        mine_ref[pair * N + N // 2 : (pair + 1) * N, :] = jnp.where(is_first, odd, even)
    for q in range(STATES):
        out_ref[q] = plain_ref[...]


def own_kernel(v_ref, a_ref, ap_ref, h3_ref, h2_ref,
               act_ref, mine_ref, other_ref, ops_ref, left_ref, wh_ref, wl_ref):
    spread(h3_ref, ops_ref)
    left = split_lanes(a_ref[...])

    def own_terms(j, carry):
        for u in range(UNROLL):
            t = j * UNROLL + u
            product = dot_nt(left, tile_nt(ops_ref[t]))
            put_term(product, [v_ref[t, g] for g in range(G)], t, wh_ref, wl_ref)
        return carry

    lax.fori_loop(0, CHUNKS, own_terms, 0)
    wide = jnp.concatenate([ap_ref[p * N : (p + 1) * N, :] for p in range(PAIRS)], axis=1)
    high, low = split(wide)
    rows_both = jnp.concatenate([high, low], axis=0)
    for j in range(CHUNKS):
        part = slice(j * UNROLL * N, (j + 1) * UNROLL * N)
        both = dot_nt(rows_both, wh_ref[part, :])
        field = both[:N] + both[N:] + dot_nt(high, wl_ref[part, :])
        for half in range(2):
            lanes = slice(half * LANES, (half + 1) * LANES)
            rows = slice((2 * j + half) * N // 2, (2 * j + half + 1) * N // 2)
            mine_ref[rows, :] = field[: N // 2, lanes]
            other_ref[rows, :] = field[N // 2 :, lanes]

    spread(h2_ref, ops_ref)
    for i in range(OWN_TILES):
        put_left((ops_ref[2 * i], ops_ref[2 * i + 1]), i, left_ref)
    act_ref[...] = act_on(left_ref, wh_ref, wl_ref)


def turned_kernel(cv_ref, ap_ref, c3_ref, zh0_ref, zl0_ref, zh_hbm, zl_hbm,
                  ops_ref, zh_ref, zl_ref, sems):
    def chunk_copies(j):
        rows = pl.ds(pl.multiple_of(j * UNROLL * N, UNROLL * N), UNROLL * N)
        return [
            pltpu.make_async_copy(zh_ref.at[rows, :], zh_hbm.at[rows, :], sems.at[0, j]),
            pltpu.make_async_copy(zl_ref.at[rows, :], zl_hbm.at[rows, :], sems.at[1, j]),
        ]

    left_p = split_lanes(ap_ref[...])
    spread(c3_ref, ops_ref)

    def coupling_term(k, high_ref, low_ref, index):
        product = dot(left_p, tile_nn(ops_ref[k]))
        put_term(product, [cv_ref[k, g] for g in range(G)], index, high_ref, low_ref)

    def sent_terms(j, carry):
        for u in range(UNROLL):
            coupling_term(HELD_TERMS + j * UNROLL + u, zh_ref, zl_ref, j * UNROLL + u)

        @pl.when(j > 0)
        def _():
            for copy in chunk_copies(j - 1):
                copy.start()

        return carry

    def held_terms(j, carry):
        for u in range(UNROLL):
            coupling_term(j * UNROLL + u, zh0_ref, zl0_ref, j * UNROLL + u)
        return carry

    lax.fori_loop(0, SENT_CHUNKS, sent_terms, 0)
    lax.fori_loop(0, 1, held_terms, 0)
    for copy in chunk_copies(SENT_CHUNKS - 1):
        copy.start()
    lax.fori_loop(1, HELD_TERMS // UNROLL, held_terms, 0)
    for j in range(SENT_CHUNKS):
        for copy in chunk_copies(j):
            copy.wait()


def field_kernel(source_ref, term_ref, valid_ref, all_ref, zh0_ref, zl0_ref, zh_hbm, zl_hbm,
                 mine_ref, other_ref, both_ref, zh_ref, zl_ref, sems):
    held = HELD_TERMS * N
    copies = []
    for j in range(SENT_CHUNKS):
        rows = pl.ds(j * UNROLL * N, UNROLL * N)
        to_rows = pl.ds(held + j * UNROLL * N, UNROLL * N)
        copies += [
            pltpu.make_async_copy(zh_hbm.at[rows, :], zh_ref.at[to_rows, :], sems.at[0, j]),
            pltpu.make_async_copy(zl_hbm.at[rows, :], zl_ref.at[to_rows, :], sems.at[1, j]),
        ]
    for copy in copies:
        copy.start()
    zh_ref[:held, :] = zh0_ref[...]
    zl_ref[:held, :] = zl0_ref[...]
    for q in range(STATES):
        for pair in range(PAIRS):
            high, low = split(all_ref[q, pair * N : (pair + 1) * N, :])
            lanes = slice(pair * LANES, (pair + 1) * LANES)
            both_ref[q, :N, lanes] = high
            both_ref[q, N:, lanes] = low
    for copy in copies:
        copy.wait()
    left_lanes = is_left(N)

    def slot_field(slot):
        rows = pl.ds(pl.multiple_of(term_ref[slot] * N, N), N)
        z = jnp.concatenate([zh_ref[rows, :], zl_ref[rows, :]], axis=0)
        product = dot_nt(z, both_ref[source_ref[slot]])
        half = product[:N] + product[N:]
        field = half + pltpu.roll(half, N, 1)
        return jnp.where(valid_ref[slot] == 1, field, 0.0)

    def slot_pairs(j, carry):
        for u in range(4):
            i = 4 * j + u
            field = jnp.where(left_lanes, slot_field(2 * i), slot_field(2 * i + 1))
            where_to = pl.ds(i, N // 2, stride=PAIR_TILES)
            mine_ref[where_to, :] = field[: N // 2]
            other_ref[where_to, :] = field[N // 2 :]
        return carry

    lax.fori_loop(0, PAIR_TILES // 4, slot_pairs, 0)


def pair_kernel(source_ref, term_ref, valid_ref, cv_ref, all_ref, c3_ref, c2_ref, act_ref,
                out_ref, left_all_ref, ops_ref, left_ref, wh_ref, wl_ref, sum_ref):
    for q in range(STATES):
        left_all_ref[q] = split_lanes(all_ref[q])
    spread(c2_ref, ops_ref)

    def left_tiles(i, carry):
        for u in range(2):
            tile = 2 * i + u
            first, second = term_ref[2 * tile], term_ref[2 * tile + 1]
            put_left((ops_ref[first], ops_ref[second]), tile, left_ref)
        return carry

    lax.fori_loop(0, SLOTS // 4, left_tiles, 0)
    spread(c3_ref, ops_ref)

    def slot_terms(j, carry):
        for u in range(UNROLL):
            slot = j * UNROLL + u
            k = term_ref[slot]
            product = dot_nt(left_all_ref[source_ref[slot]], tile_nt(ops_ref[k]))
            is_valid = valid_ref[slot] == 1
            weights = [jnp.where(is_valid, cv_ref[k, g], 0.0) for g in range(G)]
            put_term(product, weights, slot, wh_ref, wl_ref)
        return carry

    lax.fori_loop(0, SLOTS // UNROLL, slot_terms, 0)
    action = act_ref[...] + act_on(left_ref, wh_ref, wl_ref)
    left = is_left(N // 2)
    for pair in range(PAIRS):
        sum_ref[pair * N : (pair + 1) * N, :] = action[:, pair * LANES : (pair + 1) * LANES]
        even = sum_ref[pl.ds(pair * N, N // 2, stride=2), :]
        odd = sum_ref[pl.ds(pair * N + 1, N // 2, stride=2), :]
        one = jnp.where(left, even, pltpu.roll(odd, N, 1))
        two = jnp.where(left, pltpu.roll(even, N, 1), odd)
        out_ref[pl.ds(2 * pair, N // 2, stride=G), :] = one
        out_ref[pl.ds(2 * pair + 1, N // 2, stride=G), :] = two


def merge_kernel(mine_ref, theirs_ref, own_ref, out_ref):
    for a in range(N // 2):
        here = slice(a * PAIR_TILES, (a + 1) * PAIR_TILES)
        out_ref[a * ALL_TILES : a * ALL_TILES + PAIR_TILES, :] = mine_ref[here, :] + theirs_ref[here, :]
    for r in range(LAST_TILES):
        out_ref[pl.ds(PAIR_TILES + r, N // 2, stride=ALL_TILES), :] = own_ref[r]


def total_kernel(parts_ref, own_ref, pair_ref):
    def part(i, first, count):
        return parts_ref[i * ALL_TILES + first : i * ALL_TILES + first + count, :]

    total = part(0, 0, PAIR_TILES)
    for i in range(1, N // 2):
        total = total + part(i, 0, PAIR_TILES)
    pair_ref[...] = total
    for x in range(X_CHIPS):
        total = part(x, PAIR_TILES, LAST_TILES)
        for z in range(1, N // 2 // X_CHIPS):
            total = total + part(z * X_CHIPS + x, PAIR_TILES, LAST_TILES)
        own_ref[x * LAST_TILES : (x + 1) * LAST_TILES, :] = total


def shape(*dims, dtype=F32):
    return jax.ShapeDtypeStruct(dims, dtype)


def cost(flops, nbytes):
    return pl.CostEstimate(flops=flops, bytes_accessed=nbytes, transcendentals=0)


def params(mib):
    return pltpu.CompilerParams(vmem_limit_bytes=mib << 20)


OWN_GRANT = 52
FIELD_GRANT = 51


def arrange(core, raw):
    return pl.pallas_call(
        arrange_kernel,
        out_shape=(shape(STATES, PAIRS * N, LANES), shape(PAIRS * N, LANES), shape(PAIRS * N, LANES)),
        in_specs=[SMEM, VMEM],
        out_specs=[pl.BlockSpec(), VMEM, VMEM],
        compiler_params=params(8),
        name="arrange",
    )(core, raw)


def own_part(v, a2, a2p, h3, h2):
    big = pltpu.VMEM((TERMS * N, G * N), BF16)
    return pl.pallas_call(
        own_kernel,
        out_shape=(
            shape(N, G * N),
            shape(N // 2 * OWN_TILES, LANES),
            shape(N // 2 * OWN_TILES, LANES),
        ),
        in_specs=[SMEM] + [VMEM] * 4,
        out_specs=[VMEM] * 3,
        scratch_shapes=[
            pltpu.VMEM((TERMS, N, LANES), F32),
            pltpu.VMEM((LANES, TERMS * N), BF16),
            big, big,
        ],
        compiler_params=params(24),
        cost_estimate=cost(2_000_000_000, 4 << 20),
        name="own_part",
    )(v, a2, a2p, h3, h2)


def turned(cv, a2p, c3):
    big = pltpu.VMEM((SENT_TERMS * N, G * N), BF16)
    return pl.pallas_call(
        turned_kernel,
        out_shape=(
            shape(HELD_TERMS * N, G * N, dtype=BF16),
            shape(HELD_TERMS * N, G * N, dtype=BF16),
            shape(SENT_TERMS * N, G * N, dtype=BF16),
            shape(SENT_TERMS * N, G * N, dtype=BF16),
        ),
        in_specs=[SMEM] + [VMEM] * 2,
        out_specs=[VMEM] * 2 + [HBM] * 2,
        scratch_shapes=[
            pltpu.VMEM((TERMS, N, LANES), F32),
            big, big,
            pltpu.SemaphoreType.DMA((2, SENT_CHUNKS)),
        ],
        compiler_params=params(OWN_GRANT),
        cost_estimate=cost(1_000_000_000, 6 << 20),
        name="turned",
    )(cv, a2p, c3)


def pair_fields(source, term, valid, everyone, z):
    rows = N // 2 * PAIR_TILES
    return pl.pallas_call(
        field_kernel,
        out_shape=(shape(rows, LANES), shape(rows, LANES)),
        in_specs=[SMEM] * 3 + [VMEM] * 3 + [HBM] * 2,
        out_specs=[VMEM] * 2,
        scratch_shapes=[
            pltpu.VMEM((STATES, LANES, G * N), BF16),
            pltpu.VMEM((TERMS * N, G * N), BF16),
            pltpu.VMEM((TERMS * N, G * N), BF16),
            pltpu.SemaphoreType.DMA((2, SENT_CHUNKS)),
        ],
        compiler_params=params(FIELD_GRANT),
        cost_estimate=cost(3_000_000_000, 6 << 20),
        name="pair_fields",
    )(source, term, valid, everyone, *z)


def pair_action(source, term, valid, cv, everyone, c3, c2, act):
    return pl.pallas_call(
        pair_kernel,
        out_shape=shape(PAIRS * N, LANES),
        in_specs=[SMEM] * 4 + [VMEM] * 4,
        out_specs=pl.BlockSpec(),
        scratch_shapes=[
            pltpu.VMEM((STATES, PAIRS * N, 2 * LANES), BF16),
            pltpu.VMEM((TERMS, N, LANES), F32),
            pltpu.VMEM((LANES, SLOTS * N), BF16),
            pltpu.VMEM((SLOTS * N, G * N), BF16),
            pltpu.VMEM((SLOTS * N, G * N), BF16),
            pltpu.VMEM((PAIRS * N, LANES), F32),
        ],
        compiler_params=params(24),
        cost_estimate=cost(3_000_000_000, 4 << 20),
        name="pair_action",
    )(source, term, valid, cv, everyone, c3, c2, act)


def merge(mine, theirs, own):
    return pl.pallas_call(
        merge_kernel,
        out_shape=shape(N // 2 * ALL_TILES, LANES),
        in_specs=[VMEM] * 3,
        out_specs=pl.BlockSpec(),
        compiler_params=params(8),
        name="merge",
    )(mine, theirs, own)


def total(parts):
    return pl.pallas_call(
        total_kernel,
        out_shape=(shape(OWN_TILES, LANES), shape(PAIR_TILES, LANES)),
        in_specs=[pl.BlockSpec()],
        out_specs=(pl.BlockSpec(), pl.BlockSpec()),
        compiler_params=params(8),
        name="total",
    )(parts)


def tile_rows(flat):
    blocks = flat.shape[0] // 8
    tiles = flat.reshape(blocks, 8, N // 2, LANES)
    return tiles.transpose(0, 2, 1, 3).reshape(blocks * 8 * N // 2, LANES)


def read_list(pairs, myself):
    is_mine = pairs[:, 0] == myself
    rank = jnp.cumsum(is_mine.astype(jnp.int32)) - 1
    slots = jnp.arange(SLOTS, dtype=jnp.int32)
    picked = (rank[None, :] == slots[:, None]) & is_mine[None, :]
    source = jnp.sum(jnp.where(picked, pairs[None, :, 1], 0), axis=1)
    term = jnp.sum(jnp.where(picked, pairs[None, :, 2], 0), axis=1)
    valid = jnp.sum(picked.astype(jnp.int32), axis=1)
    return source, term, valid


def other_core(value):
    return lax.ppermute(value, "core", [(0, 1), (1, 0)])


def reduce_own(mine, other):
    x = lax.axis_index("x")
    tiles = (mine + other_core(other)).reshape(2, 2, LAST_TILES, N // 2, LANES)
    for axis, bit in ((1, 1), (0, 2)):
        mine_here = (x // bit) % 2
        keep = lax.dynamic_index_in_dim(tiles, mine_here, axis, False)
        send = lax.dynamic_index_in_dim(tiles, 1 - mine_here, axis, False)
        tiles = keep + lax.ppermute(send, "x", [(i, i ^ bit) for i in range(X_CHIPS)])
    return tiles


def per_device(coeffs, diag_h2, diag_h3, diag_v1, coup_h2, coup_h3, coup_v1, pairs):
    core = lax.axis_index("core").astype(jnp.int32)[None]
    to_all, plain, mine_first = arrange(core, tile_rows(coeffs[0]))
    everyone = lax.all_to_all(to_all, "state", 0, 0, tiled=True)
    listed = read_list(pairs, lax.axis_index("state"))
    c3 = tile_rows(coup_h3)
    act, own_mine, own_other = own_part(
        diag_v1[0], plain, mine_first, tile_rows(diag_h3[0]), tile_rows(diag_h2[0])
    )
    z = turned(coup_v1, mine_first, c3)
    everyone, own_columns = lax.optimization_barrier(
        (everyone, reduce_own(own_mine, own_other))
    )
    pair_mine, pair_other = pair_fields(*listed, everyone, z)
    sums = merge(pair_mine, other_core(pair_other), own_columns)
    parts = lax.all_to_all(
        sums.reshape(N // 2, 1, ALL_TILES * LANES), ("z", "x"), 0, 0, tiled=True
    )
    out = pair_action(*listed, coup_v1, everyone, c3, tile_rows(coup_h2), act)
    action = out.reshape(N // 2, G, LANES).transpose(1, 0, 2).reshape(1, G, N * N)
    own_row, pair_row = total(parts.reshape(N // 2 * ALL_TILES, LANES))
    return action, own_row.reshape(1, 1, TERMS * N), pair_row.reshape(1, 1, SLOTS * N)


def solution(mesh):
    fine = Mesh(mesh.devices.reshape(8, 8, 4, 2), ("state", "z", "x", "core"))
    mode = ("z", "x", "core")
    placed = (
        P("state", mode, None),
        P("state", None, None),
        P("state", None, None),
        P("state", None, mode),
        P(),
        P(),
        P(None, mode),
        P(),
    )
    out = P("state", mode, None)
    return jax.shard_map(
        per_device, mesh=fine, in_specs=placed, out_specs=(out, out, out), check_vma=False
    )
```
